256 devices in a mesh: box: 256 (over z, y, x, core).
Axes of the slice: x: 4, y: 4, z: 8, core: 2. Of those that a mesh axis runs over, the one named last changes fastest.
Arguments:
- fine_mult: bfloat16 [262144, 128], P('box'), may hold values from -6 to 6
- parent_mult: bfloat16 [32768, 128], P('box'), may hold values from -6 to 6
- fine_mask: int32 [20, 262144], P(None, 'box'), may hold values from 0 to 65535, as said below
- parent_mask: int32 [20, 32768], P(None, 'box'), may hold values from 0 to 65535, as said below
- kernels: bfloat16 [316, 128, 128], replicated, may hold values from -0.0390625 to 0.0390625
- shift_ops: bfloat16 [8, 128, 128], replicated, may hold values from -0.5 to 0.5
Outputs:
- fine_local: bfloat16 [262144, 128], P('box')
- parent_local: bfloat16 [32768, 128], P('box')
The draws below stay inside these ranges and needn't reach their ends.
Inputs may be any that keep to these rules, and one draw needn't show every extreme that they name: `fine_mask`: bit d mod 16 of word floor(d / 16) of box t is set only where the box at t's coordinates plus offset d lies inside the grid and its parent is one of the 27 boxes around t's parent; bits 12 to 15 of word 19 are zero; sources in many regions are missing from the lists. `parent_mask`: the same rule at the parent level.
All inputs are finite; a program needn't handle non-finite values.
Results may differ from the reference program's by a relative error of at most 0.0027.
Values may be sent and summed in bfloat16 or wider, within the bound.
No kernel may reach another device: no remote copies, remote signals or barrier semaphores. Data moves between devices by JAX's collectives and lax.ppermute only.
A program may use at most 320 MiB of HBM per device.

```python
import jax
import jax.numpy as jnp
import numpy as np
from jax import lax

R = 128
DIRS = 316
BOXES = 262144
PBOXES = 32768


def direction_table_drawn():
    listing = []
    for group_first in range(3):
        for group_second in range(3):
            for group_third in range(3):
                ranges_all = []
                for marker in (group_first, group_second, group_third):
                    if marker == 0:
                        ranges_all.append([-2, -1, 0, 1, 2])
                    elif marker == 1:
                        ranges_all.append([-3])
                    else:
                        ranges_all.append([3])
                for along_one in ranges_all[0]:
                    for along_two in ranges_all[1]:
                        for along_three in ranges_all[2]:
                            if max(abs(along_one), abs(along_two), abs(along_three)) >= 2:
                                listing.append((along_one, along_two, along_three, group_first, group_second, group_third))
    return np.array(listing, np.int32)


def packed_lists(key, box_count):
    total_bits = box_count.bit_length() - 1
    positions = jnp.arange(box_count, dtype=jnp.int32)
    coords = [jnp.zeros((box_count,), jnp.int32) for dim_code in range(3)]
    domain = [1, 1, 1]
    for position in range(total_bits):
        dim_code = 2 - position % 3
        coords[dim_code] = coords[dim_code] + jnp.left_shift(jnp.right_shift(positions, position) & 1, position // 3)
        domain[dim_code] = domain[dim_code] * 2
    region_bits = min(6, total_bits)
    regions = jnp.right_shift(positions, total_bits - region_bits)
    region_levels = jax.random.randint(jax.random.fold_in(key, 1), (2 ** region_bits,), 1, 5)
    occupied = jax.random.randint(jax.random.fold_in(key, 2), (box_count,), 0, 4) < region_levels[regions]
    offsets_table = direction_table_drawn()
    packed = [jnp.zeros((box_count,), jnp.int32) for word_number in range(20)]
    for number in range(offsets_table.shape[0]):
        inside_all = jnp.ones((box_count,), bool)
        near_all = jnp.ones((box_count,), bool)
        shifted = []
        for dim_code in range(3):
            moved = coords[dim_code] + int(offsets_table[number, dim_code])
            inside_all = inside_all & (moved >= 0) & (moved < domain[dim_code])
            parent_gap = jnp.right_shift(moved, 1) - jnp.right_shift(coords[dim_code], 1)
            near_all = near_all & (parent_gap >= -1) & (parent_gap <= 1)
            shifted.append(moved)
        source_index = jnp.zeros((box_count,), jnp.int32)
        for position in range(total_bits):
            dim_code = 2 - position % 3
            source_index = source_index + jnp.left_shift(jnp.right_shift(shifted[dim_code], position // 3) & 1, position)
        source_index = jnp.where(inside_all, source_index, 0)
        bit_value = (inside_all & near_all & occupied[source_index]).astype(jnp.int32)
        packed[number // 16] = packed[number // 16] + jnp.left_shift(bit_value, number % 16)
    return jnp.stack(packed)


def draw_fine_mask(key, part):
    return packed_lists(jax.random.fold_in(key, 11), BOXES)


def draw_parent_mask(key, part):
    return packed_lists(jax.random.fold_in(key, 12), PBOXES)


def block_scale(key, dims, shards, low, top_value):
    gain, own = 1.0, jax.random.fold_in(key, 6)
    for axis_at, shards_of in shards:
        draws = jnp.exp(jax.random.uniform(jax.random.fold_in(own, axis_at), (shards_of,), jnp.float32, low / len(shards), top_value / len(shards)))
        gain = gain * jnp.repeat(draws, dims[axis_at] // shards_of).reshape([-1 if axis == axis_at else 1 for axis in range(len(dims))])
    return gain


def bell_draw(stream_key, shape, width, most, split=(), held_as=jnp.bfloat16):
    values = width * jax.random.normal(stream_key, shape, jnp.float32)
    if split:
        values = values * block_scale(stream_key, shape, split, -0.22, 0.18)
    return jnp.clip(values, -most, most).astype(held_as)


def setup_inputs(seed: int = 0) -> dict:
    arg_keys = jax.random.split(jax.random.key(seed), 7)
    return {
        "fine_mult": bell_draw(arg_keys[0], (BOXES, R), 1.0, 6.0, ((0, 256),)),
        "parent_mult": bell_draw(arg_keys[1], (PBOXES, R), 1.0, 6.0, ((0, 256),)),
        "fine_mask": draw_fine_mask(jax.random.fold_in(arg_keys[6], 71), 0),
        "parent_mask": draw_parent_mask(jax.random.fold_in(arg_keys[6], 71), 0),
        "kernels": bell_draw(arg_keys[4], (DIRS, R, R), (R * 189) ** -0.5, 0.0390625),
        "shift_ops": bell_draw(arg_keys[5], (8, R, R), R ** -0.5, 0.5),
    }


def direction_table():
    listing = []
    for group_first in range(3):
        for group_second in range(3):
            for group_third in range(3):
                ranges_all = []
                for marker in (group_first, group_second, group_third):
                    if marker == 0:
                        ranges_all.append([-2, -1, 0, 1, 2])
                    elif marker == 1:
                        ranges_all.append([-3])
                    else:
                        ranges_all.append([3])
                for along_one in ranges_all[0]:
                    for along_two in ranges_all[1]:
                        for along_three in ranges_all[2]:
                            if max(abs(along_one), abs(along_two), abs(along_three)) >= 2:
                                listing.append((along_one, along_two, along_three, group_first, group_second, group_third))
    return np.array(listing, np.int32)


def grid_order(total_bits):
    axes_order = []
    extents = []
    for target in range(3):
        chosen = [position for position in range(total_bits - 1, -1, -1) if 2 - position % 3 == target]
        axes_order += [total_bits - 1 - position for position in chosen]
        extents.append(2 ** len(chosen))
    return axes_order, extents


def to_grid(morton_rows, total_bits):
    axes_order, extents = grid_order(total_bits)
    trailing = morton_rows.shape[1:]
    bitwise = morton_rows.reshape((2,) * total_bits + trailing)
    permuted = jnp.transpose(bitwise, tuple(axes_order) + tuple(range(total_bits, total_bits + len(trailing))))
    return permuted.reshape(tuple(extents) + trailing)


def from_grid(gridded, total_bits):
    axes_order, extents = grid_order(total_bits)
    trailing = gridded.shape[3:]
    bitwise = gridded.reshape((2,) * total_bits + trailing)
    inverse = [0] * total_bits
    for position, source in enumerate(axes_order):
        inverse[source] = position
    permuted = jnp.transpose(bitwise, tuple(inverse) + tuple(range(total_bits, total_bits + len(trailing))))
    return permuted.reshape((2 ** total_bits,) + trailing)


def level_sum(mult, packed, kernels, factor):
    level_bits = mult.shape[0].bit_length() - 1
    rank_width = mult.shape[1]
    gridded = to_grid(mult, level_bits)
    padded = jnp.pad(gridded, ((3, 3), (3, 3), (3, 3), (0, 0)))
    word_grid = to_grid(jnp.transpose(packed), level_bits)
    offsets_table = jnp.asarray(direction_table()[:, :3])
    numbers = jnp.arange(kernels.shape[0], dtype=jnp.int32)
    extents = tuple(gridded.shape[:3])
    zero_index = jnp.zeros((), jnp.int32)

    def one_direction(accumulated, inputs):
        kernel, offset, number = inputs
        starts = (3 + offset[0], 3 + offset[1], 3 + offset[2], zero_index)
        window = lax.dynamic_slice(padded, starts, extents + (rank_width,))
        word_slice = lax.dynamic_index_in_dim(word_grid, number // 16, axis=3, keepdims=False)
        present = (jnp.right_shift(word_slice, number % 16) & 1).astype(jnp.bfloat16)
        masked = (window * present[..., None]).reshape(-1, rank_width)
        product = jnp.dot(masked.astype(jnp.float32), kernel.astype(jnp.float32), preferred_element_type=jnp.float32)
        return accumulated + product.reshape(accumulated.shape), None

    start_value = jnp.zeros(extents + (rank_width,), jnp.float32)
    accumulated, unused = lax.scan(one_direction, start_value, (kernels, offsets_table, numbers))
    return from_grid(accumulated * factor, level_bits)


def reference(fine_mult, parent_mult, fine_mask, parent_mask, kernels, shift_ops):
    parent_local = level_sum(parent_mult, parent_mask, kernels, 0.5).astype(jnp.bfloat16)
    rank_width = fine_mult.shape[1]
    translated = jnp.einsum("pr,krs->pks", parent_local.astype(jnp.float32), shift_ops.astype(jnp.float32))
    translated = translated.reshape(fine_mult.shape[0], rank_width)
    fine_total = level_sum(fine_mult, fine_mask, kernels, 1.0) + translated
    return (fine_total.astype(jnp.bfloat16), parent_local)
```

```python
import jax
import jax.numpy as jnp
import numpy as np
from jax import lax
from jax.experimental import pallas as pl
from jax.experimental.pallas import tpu as pltpu
from jax.sharding import PartitionSpec as P

DIM_OF_BIT = (2, 1, 0)


def direction_table():
    listing = []
    picks = ([-2, -1, 0, 1, 2], [-3], [3])
    for ga in range(3):
        for gb in range(3):
            for gc in range(3):
                for oa in picks[ga]:
                    for ob in picks[gb]:
                        for oc in picks[gc]:
                            if max(abs(oa), abs(ob), abs(oc)) >= 2:
                                listing.append((oa, ob, oc, ga, gb, gc))
    return np.array(listing, np.int32)


def grid_order(total_bits):
    axes_order = []
    extents = []
    for target in range(3):
        chosen = [k for k in range(total_bits - 1, -1, -1) if 2 - k % 3 == target]
        axes_order += [total_bits - 1 - k for k in chosen]
        extents.append(2 ** len(chosen))
    return axes_order, extents


def to_grid(rows, total_bits):
    axes_order, extents = grid_order(total_bits)
    trailing = rows.shape[1:]
    bitwise = rows.reshape((2,) * total_bits + trailing)
    extra = tuple(range(total_bits, total_bits + len(trailing)))
    return jnp.transpose(bitwise, tuple(axes_order) + extra).reshape(tuple(extents) + trailing)


def grid_permutation(total_bits):
    axes_order, _ = grid_order(total_bits)
    numbers = np.arange(2**total_bits).reshape((2,) * total_bits)
    return np.transpose(numbers, axes_order).reshape(-1)


def octant_grids(rows, total_bits):
    width = rows.shape[1]
    parents = to_grid(rows.reshape(-1, 8, width), total_bits - 3)
    return jnp.moveaxis(parents, 3, 0)


def owned_bits(dim, low_bits, device_bits):
    return [k for k in range(device_bits) if 2 - (low_bits + k) % 3 == dim]


def pair_route(dim, odd, low_bits, device_bits):
    bits = owned_bits(dim, low_bits, device_bits)
    route = []
    for number in range(2**device_bits):
        place = sum(((number >> bit) & 1) << k for k, bit in enumerate(bits))
        other = place + (1 if place % 2 == odd else -1)
        if 0 <= other < 2 ** len(bits):
            target = number
            for k, bit in enumerate(bits):
                target = target & ~(1 << bit) | ((other >> k) & 1) << bit
            route.append((number, target))
    return route


def exchange(fine, parent, dim, low_bits, device_index, device_bits):
    first_bit = owned_bits(dim, low_bits, device_bits)[0]
    is_odd = (jnp.right_shift(device_index, first_bit) & 1) == 1
    axis = dim + 1

    def face(block, last):
        at = block.shape[axis] - 1 if last else 0
        return lax.index_in_dim(block, at, axis, keepdims=False)

    def packed(last):
        pieces = [face(b, last).reshape(8, -1, b.shape[-1]) for b in (fine, parent)]
        return jnp.concatenate(pieces, axis=1)

    top = packed(True)
    bottom = packed(False)
    even_send = jnp.where(is_odd, bottom, top)
    odd_send = jnp.where(is_odd, top, bottom)
    odd_got = lax.ppermute(odd_send, "box", pair_route(dim, 1, low_bits, device_bits))
    even_got = lax.ppermute(even_send, "box", pair_route(dim, 0, low_bits, device_bits))
    below = jnp.where(is_odd, even_got, odd_got)
    above = jnp.where(is_odd, odd_got, even_got)
    split = face(fine, True).size // (8 * fine.shape[-1])
    out = []
    for block, pick in ((fine, slice(0, split)), (parent, slice(split, None))):
        shape = face(block, True).shape
        low = jnp.expand_dims(below[:, pick].reshape(shape), axis)
        high = jnp.expand_dims(above[:, pick].reshape(shape), axis)
        out.append(jnp.concatenate([low, block, high], axis=axis))
    return out


def tables(fine_rows, slab_rows):
    offsets = direction_table()
    count = offsets.shape[0]
    fine_at = np.zeros((8, count), np.int32)
    parent_at = np.zeros((8, count), np.int32)
    for octant in range(8):
        parity = np.array([octant >> 2 & 1, octant >> 1 & 1, octant & 1])
        moved = offsets[:, :3] + parity
        source = moved & 1
        shift = np.clip((moved >> 1) + 1, 0, 2)
        source_octant = source[:, 0] * 4 + source[:, 1] * 2 + source[:, 2]
        fine_at[octant] = (
            (shift[:, 1] * 3 + shift[:, 2]) * 8 + source_octant
        ) * fine_rows + shift[:, 0] * slab_rows
        parent_at[octant] = (
            (shift[:, 0] * 3 + shift[:, 1]) * 3 + shift[:, 2]
        ) * 8 + source_octant
    return fine_at, parent_at


def group_lists():
    offsets = direction_table()
    runs = []
    start = 0
    for number in range(1, offsets.shape[0] + 1):
        if number == offsets.shape[0] or tuple(offsets[number, 3:]) != tuple(offsets[start, 3:]):
            markers = [int(v) for v in offsets[start, 3:]]
            octants = []
            for octant in range(8):
                parity = (octant >> 2 & 1, octant >> 1 & 1, octant & 1)
                if all(m == 0 or (m == 1 and p == 1) or (m == 2 and p == 0) for m, p in zip(markers, parity)):
                    octants.append(octant)
            runs.append((start, number, octants))
            start = number
    return runs


def make_kernel(F, G, words, classes, copies):
    rows = F + G

    def kernel(fine_at, parent_at, starts, octs, masks, x, xp, kern, shift, perm, fine_out,
               parent_out, wbuf, mbuf, lhs, acc, sems):
        loads = []
        for number, (lo, hi) in enumerate(copies):
            cp = pltpu.make_async_copy(kern.at[pl.ds(lo * 128, (hi - lo) * 128)],
                                       wbuf.at[pl.ds(lo * 128, (hi - lo) * 128)], sems.at[number])
            cp.start()
            loads.append(cp)

        def spread(p, carry):
            for w in range(words):
                column = masks[p, :, w : w + 1]
                mbuf[w, p] = jnp.broadcast_to(column, (rows, 128)).astype(jnp.int16)
            return carry

        lax.fori_loop(0, 8, spread, 0)
        acc[...] = jnp.zeros_like(acc)

        def fill(slot, octant, d, column):
            word = d // 16
            bit = jnp.left_shift(1, d % 16)
            wanted = jnp.broadcast_to(bit, (16, 128)).astype(jnp.int16)
            zero = jnp.zeros((16, 128), jnp.bfloat16)
            none = jnp.zeros((16, 128), jnp.int16)
            at_f = pl.multiple_of(fine_at[octant, d], 16)
            at_p = parent_at[octant, d]
            for r in range(rows // 16):
                held = mbuf[word, octant, r * 16 : r * 16 + 16, :]
                if r * 16 < F:
                    value = x[pl.ds(pl.multiple_of(at_f + r * 16, 16), 16), :]
                else:
                    value = xp[at_p]
                kept = jnp.where((held & wanted) != none, value, zero)
                lhs[slot * rows + r * 16 : slot * rows + r * 16 + 16, column * 128 : column * 128 + 128] = kept

        def run_class(first_table, chunk, lanes):
            def step(number, carry):
                d0 = starts[number]
                for j in range(chunk):
                    for i in range(lanes):
                        octant = i if lanes == 8 else octs[number, i]
                        fill(i, octant, d0 + j, j)
                weights = wbuf[pl.ds(pl.multiple_of(d0 * 128, 128), chunk * 128), :]
                got = jnp.dot(lhs[: lanes * rows, : chunk * 128], weights, preferred_element_type=jnp.float32)
                for i in range(lanes):
                    octant = i if lanes == 8 else octs[number, i]
                    acc[octant] += got[i * rows : (i + 1) * rows]
                return carry

            return step

        done = 0
        for lanes, chunk, first, last, ready in classes:
            while done < ready:
                loads[done].wait()
                done += 1
            lax.fori_loop(first, last, run_class(first, chunk, lanes), 0)

        far = []
        for p in range(8):
            far.append((acc[p, F:, :] * 0.5).astype(jnp.bfloat16))
        local = jnp.concatenate(far, axis=0)
        parent_out[...] = local
        ordered = jnp.dot(perm[...], local, preferred_element_type=jnp.float32).astype(jnp.bfloat16)
        for p in range(8):
            moved = jnp.dot(ordered, shift[p], preferred_element_type=jnp.float32)
            fine_out[p] = (acc[p, :F, :] + moved).astype(jnp.bfloat16)

    return kernel


def on_device(fine_mult, parent_mult, fine_mask, parent_mask, kernels, shift_ops):
    device_bits = lax.axis_size("box").bit_length() - 1
    device_index = lax.axis_index("box")
    fine_bits = fine_mult.shape[0].bit_length() - 1
    parent_bits = parent_mult.shape[0].bit_length() - 1
    width = fine_mult.shape[1]
    count = kernels.shape[0]
    words = fine_mask.shape[0]
    fine = octant_grids(fine_mult, fine_bits)
    parent = octant_grids(parent_mult, parent_bits)
    F = fine_mult.shape[0] // 8
    G = parent_mult.shape[0] // 8
    n1, n2, n3 = fine.shape[1:4]
    m1, m2, m3 = parent.shape[1:4]
    masks = jnp.concatenate(
        [
            octant_grids(fine_mask.T, fine_bits).reshape(8, F, words),
            octant_grids(parent_mask.T, parent_bits).reshape(8, G, words),
        ],
        axis=1,
    )
    for dim in (1, 2, 0):
        fine, parent = exchange(fine, parent, dim, fine_bits, device_index, device_bits)
    x = jnp.stack(
        [
            fine[:, :, b : b + n2, c : c + n3].reshape(8, -1, width)
            for b in range(3)
            for c in range(3)
        ]
    ).reshape(-1, width)
    xp = jnp.stack(
        [
            parent[:, a : a + m1, b : b + m2, c : c + m3].reshape(8, G, width)
            for a in range(3)
            for b in range(3)
            for c in range(3)
        ]
    ).reshape(-1, G, width)
    fine_at, parent_at = tables((n1 + 2) * n2 * n3, n2 * n3)
    runs = group_lists()
    starts = []
    octs = []
    classes = []
    bounds = [0, 98, 173, 248, count]
    copies = list(zip(bounds[:-1], bounds[1:]))
    for lanes, chunk in ((8, 7), (4, 5), (2, 5), (1, 1)):
        first = len(starts)
        for lo, hi, octants in runs:
            if len(octants) == lanes:
                for at in range(lo, hi, chunk):
                    starts.append(at)
                    octs.append((octants + [0] * 8)[:8])
        classes.append((lanes, chunk, first, len(starts), 1 if lanes == 8 else len(copies)))
    parent_numbers = np.arange(parent_mult.shape[0]).reshape(-1, 8)
    order_pg = grid_permutation(parent_bits - 3)
    held = parent_numbers[order_pg].T.reshape(-1)
    wanted = grid_permutation(parent_bits)
    place = np.zeros(parent_mult.shape[0], np.int64)
    place[held] = np.arange(parent_mult.shape[0])
    perm = np.zeros((F, F), np.float32)
    perm[np.arange(F), place[wanted]] = 1
    rows = F + G
    vmem = pl.BlockSpec(memory_space=pltpu.VMEM)
    smem = pl.BlockSpec(memory_space=pltpu.SMEM)
    fine_local, parent_local = pl.pallas_call(
        make_kernel(F, G, words, classes, copies),
        out_shape=(
            jax.ShapeDtypeStruct((8, F, width), jnp.bfloat16),
            jax.ShapeDtypeStruct((8 * G, width), jnp.bfloat16),
        ),
        in_specs=[smem, smem, smem, smem, vmem, vmem, vmem, pl.BlockSpec(memory_space=pl.ANY), vmem, vmem],
        out_specs=(vmem, vmem),
        scratch_shapes=[
            pltpu.VMEM((count * width, width), jnp.bfloat16),
            pltpu.VMEM((words, 8, rows, 128), jnp.int16),
            pltpu.VMEM((8 * rows, 7 * width), jnp.bfloat16),
            pltpu.VMEM((8, rows, width), jnp.float32),
            pltpu.SemaphoreType.DMA((len(copies),)),
        ],
        compiler_params=pltpu.CompilerParams(vmem_limit_bytes=48 << 20),
        name="translate",
    )(
        jnp.asarray(fine_at),
        jnp.asarray(parent_at),
        jnp.asarray(np.array(starts, np.int32)),
        jnp.asarray(np.array(octs, np.int32)),
        masks,
        x,
        xp,
        kernels.reshape(-1, width),
        shift_ops,
        jnp.asarray(perm, jnp.bfloat16),
    )
    back_f = np.argsort(grid_permutation(fine_bits - 3))
    back_g = np.argsort(grid_permutation(parent_bits - 3))
    del back_f, back_g
    fine_local = from_octants(fine_local, fine_bits)
    parent_local = from_octants(parent_local.reshape(8, G, width), parent_bits)
    return fine_local, parent_local


def from_octants(blocks, total_bits):
    width = blocks.shape[-1]
    axes_order, extents = grid_order(total_bits - 3)
    bits = total_bits - 3
    grid = blocks.reshape((8,) + (2,) * bits + (width,))
    inverse = [0] * bits
    for position, source in enumerate(axes_order):
        inverse[source] = position
    moved = jnp.transpose(grid, tuple(1 + v for v in inverse) + (0, bits + 1))
    return moved.reshape(2**total_bits, width)


def solution(mesh):
    return jax.shard_map(
        on_device,
        mesh=mesh,
        in_specs=(P("box", None), P("box", None), P(None, "box"), P(None, "box"), P(), P()),
        out_specs=(P("box", None), P("box", None)),
        check_vma=False,
    )
```

```python
import jax
import jax.numpy as jnp
import numpy as np
from jax import lax
from jax.experimental import pallas as pl
from jax.experimental.pallas import tpu as pltpu
from jax.sharding import PartitionSpec as P

DIM_OF_BIT = (2, 1, 0)


def direction_table():
    listing = []
    picks = ([-2, -1, 0, 1, 2], [-3], [3])
    for ga in range(3):
        for gb in range(3):
            for gc in range(3):
                for oa in picks[ga]:
                    for ob in picks[gb]:
                        for oc in picks[gc]:
                            if max(abs(oa), abs(ob), abs(oc)) >= 2:
                                listing.append((oa, ob, oc, ga, gb, gc))
    return np.array(listing, np.int32)


def grid_order(total_bits):
    axes_order = []
    extents = []
    for target in range(3):
        chosen = [k for k in range(total_bits - 1, -1, -1) if 2 - k % 3 == target]
        axes_order += [total_bits - 1 - k for k in chosen]
        extents.append(2 ** len(chosen))
    return axes_order, extents


def to_grid(rows, total_bits):
    axes_order, extents = grid_order(total_bits)
    trailing = rows.shape[1:]
    bitwise = rows.reshape((2,) * total_bits + trailing)
    extra = tuple(range(total_bits, total_bits + len(trailing)))
    return jnp.transpose(bitwise, tuple(axes_order) + extra).reshape(tuple(extents) + trailing)


def grid_permutation(total_bits):
    axes_order, _ = grid_order(total_bits)
    numbers = np.arange(2**total_bits).reshape((2,) * total_bits)
    return np.transpose(numbers, axes_order).reshape(-1)


def octant_grids(rows, total_bits):
    width = rows.shape[1]
    parents = to_grid(rows.reshape(-1, 8, width), total_bits - 3)
    return jnp.moveaxis(parents, 3, 0)


def owned_bits(dim, low_bits, device_bits):
    return [k for k in range(device_bits) if 2 - (low_bits + k) % 3 == dim]


def pair_route(dim, odd, low_bits, device_bits):
    bits = owned_bits(dim, low_bits, device_bits)
    route = []
    for number in range(2**device_bits):
        place = sum(((number >> bit) & 1) << k for k, bit in enumerate(bits))
        other = place + (1 if place % 2 == odd else -1)
        if 0 <= other < 2 ** len(bits):
            target = number
            for k, bit in enumerate(bits):
                target = target & ~(1 << bit) | ((other >> k) & 1) << bit
            route.append((number, target))
    return route


def face(block, axis, last):
    at = block.shape[axis] - 1 if last else 0
    return lax.index_in_dim(block, at, axis, keepdims=False)


def packed_face(fine, parent, axis, last):
    pieces = [face(b, axis, last).reshape(8, -1, b.shape[-1]) for b in (fine, parent)]
    return jnp.concatenate(pieces, axis=1)


def parity(dim, low_bits, device_index, device_bits):
    first_bit = owned_bits(dim, low_bits, device_bits)[0]
    return (jnp.right_shift(device_index, first_bit) & 1) == 1


def exchange(fine, parent, dim, low_bits, device_index, device_bits):
    is_odd = parity(dim, low_bits, device_index, device_bits)
    axis = dim + 1
    top = packed_face(fine, parent, axis, True)
    bottom = packed_face(fine, parent, axis, False)
    even_send = jnp.where(is_odd, bottom, top)
    odd_send = jnp.where(is_odd, top, bottom)
    odd_got = lax.ppermute(odd_send, "box", pair_route(dim, 1, low_bits, device_bits))
    even_got = lax.ppermute(even_send, "box", pair_route(dim, 0, low_bits, device_bits))
    below = jnp.where(is_odd, even_got, odd_got)
    above = jnp.where(is_odd, odd_got, even_got)
    split = face(fine, axis, True).size // (8 * fine.shape[-1])
    out = []
    for block, pick in ((fine, slice(0, split)), (parent, slice(split, None))):
        shape = face(block, axis, True).shape
        low = jnp.expand_dims(below[:, pick].reshape(shape), axis)
        high = jnp.expand_dims(above[:, pick].reshape(shape), axis)
        out.append(jnp.concatenate([low, block, high], axis=axis))
    return out


def odd_groups(dim, low_bits, device_bits):
    paired = pair_route(dim, 1, low_bits, device_bits)
    groups = [[a, b] for a, b in paired if a < b]
    seen = {a for a, _ in paired}
    rest = [number for number in range(2**device_bits) if number not in seen]
    return groups + [[rest[k], rest[k + 1]] for k in range(0, len(rest), 2)]


def shift_lists():
    offsets = direction_table()
    lists = [[[] for _ in range(8)] for _ in range(3)]
    for octant in range(8):
        own = np.array([octant >> 2 & 1, octant >> 1 & 1, octant & 1])
        for number in range(offsets.shape[0]):
            moved = offsets[number, :3] + own
            if moved.min() < -2 or moved.max() > 3:
                continue
            shift = (moved >> 1) + 1
            source = moved & 1
            lists[shift[0]][octant].append((number, shift, source[0] * 4 + source[1] * 2 + source[2]))
    return lists


CHUNK = 18


def work_table(groups, slots, slab_count, slab_rows):
    table = np.zeros((5, 8, slots), np.int32)
    for octant in range(8):
        at = 0
        for place, per_octant in enumerate(groups):
            for number, shift, source in per_octant[octant]:
                across = shift[1] * 3 + shift[2]
                table[0, octant, at] = number
                table[1, octant, at] = (across * 8 + source) * slab_count * slab_rows + shift[0] * slab_rows
                table[2, octant, at] = (place * 9 + across) * 8 + source
                table[3, octant, at] = number // 16
                table[4, octant, at] = 1 << (number % 16)
                at += 1
    return table.reshape(5, 8 * slots)


def spread_masks(masks):
    rows, words = masks.shape[1:]

    def kernel(packed, out):
        def one(octant, carry):
            for w in range(words):
                column = packed[octant, :, w : w + 1]
                out[w, octant] = jnp.broadcast_to(column, (rows, 128)).astype(jnp.int16)
            return carry

        lax.fori_loop(0, 8, one, 0)

    vmem = pl.BlockSpec(memory_space=pltpu.VMEM)
    return pl.pallas_call(
        kernel,
        out_shape=jax.ShapeDtypeStruct((words, 8, rows, 128), jnp.int16),
        in_specs=[vmem],
        out_specs=vmem,
        compiler_params=pltpu.CompilerParams(vmem_limit_bytes=16 << 20),
        name="spread",
    )(masks)


def add_terms(table, slots, words, x, xp, kernels, acc):
    F = acc.shape[1] - xp.shape[1]
    rows = acc.shape[1]

    def masked(octant, at):
        place = octant * slots + at
        wanted = jnp.broadcast_to(table[4, place], (16, 128)).astype(jnp.int16)
        wanted = jnp.broadcast_to(wanted[:1], (rows, 128))
        row = pl.multiple_of(table[1, place], 16)
        value = jnp.concatenate([x[pl.ds(row, F), :], xp[table[2, place]]], axis=0)
        held = words[table[3, place], octant]
        return jnp.where((held & wanted) != 0, value, jnp.zeros_like(value))

    def step(number, carry):
        at = number * CHUNK
        for octant in range(8):
            left = jnp.concatenate([masked(octant, at + j) for j in range(CHUNK)], axis=1)
            right = jnp.concatenate([kernels[table[0, octant * slots + at + j]] for j in range(CHUNK)], axis=0)
            acc[octant] += jnp.dot(left, right, preferred_element_type=jnp.float32)
        return carry

    lax.fori_loop(0, slots // CHUNK, step, 0)


def first_terms(table, slots, words, x, xp, kernels):
    rows = words.shape[2]
    width = kernels.shape[1]

    def kernel(table, words, x, xp, kernels, acc):
        acc[...] = jnp.zeros_like(acc)
        add_terms(table, slots, words, x, xp, kernels, acc)

    vmem = pl.BlockSpec(memory_space=pltpu.VMEM)
    return pl.pallas_call(
        kernel,
        out_shape=jax.ShapeDtypeStruct((8, rows, width), jnp.float32),
        in_specs=[pl.BlockSpec(memory_space=pltpu.SMEM)] + [vmem] * 4,
        out_specs=vmem,
        compiler_params=pltpu.CompilerParams(vmem_limit_bytes=16 << 20),
        name="first_terms",
    )(table, words, x, xp, kernels)


def last_terms(table, slots, words, x, xp, kernels, sums, shift_ops, perm):
    rows = words.shape[2]
    width = kernels.shape[1]
    F = perm.shape[0]

    def kernel(table, words, x, xp, kernels, sums, shift, perm, fine_out, parent_out, acc):
        acc[...] = sums[...]
        add_terms(table, slots, words, x, xp, kernels, acc)
        far = [(acc[p, F:, :] * 0.5).astype(jnp.bfloat16) for p in range(8)]
        local = jnp.concatenate(far, axis=0)
        parent_out[...] = local
        ordered = jnp.dot(perm[...], local, preferred_element_type=jnp.float32).astype(jnp.bfloat16)
        for p in range(8):
            moved = jnp.dot(ordered, shift[p], preferred_element_type=jnp.float32)
            fine_out[p] = (acc[p, :F, :] + moved).astype(jnp.bfloat16)

    vmem = pl.BlockSpec(memory_space=pltpu.VMEM)
    return pl.pallas_call(
        kernel,
        out_shape=(
            jax.ShapeDtypeStruct((8, F, width), jnp.bfloat16),
            jax.ShapeDtypeStruct((8 * (rows - F), width), jnp.bfloat16),
        ),
        in_specs=[pl.BlockSpec(memory_space=pltpu.SMEM)] + [vmem] * 7,
        out_specs=(vmem, vmem),
        scratch_shapes=[pltpu.VMEM((8, rows, width), jnp.float32)],
        compiler_params=pltpu.CompilerParams(vmem_limit_bytes=16 << 20),
        name="last_terms",
    )(table, words, x, xp, kernels, sums, shift_ops, perm)


def parent_order(parent_bits):
    count = 2**parent_bits
    held = np.arange(count).reshape(-1, 8)[grid_permutation(parent_bits - 3)].T.reshape(-1)
    place = np.zeros(count, np.int64)
    place[held] = np.arange(count)
    perm = np.zeros((count, count), np.float32)
    perm[np.arange(count), place[grid_permutation(parent_bits)]] = 1
    return perm


def on_device(fine_mult, parent_mult, fine_mask, parent_mask, kernels, shift_ops):
    device_bits = lax.axis_size("box").bit_length() - 1
    device_index = lax.axis_index("box")
    fine_bits = fine_mult.shape[0].bit_length() - 1
    parent_bits = parent_mult.shape[0].bit_length() - 1
    width = fine_mult.shape[1]
    words = fine_mask.shape[0]
    fine = octant_grids(fine_mult, fine_bits)
    parent = octant_grids(parent_mult, parent_bits)
    F = fine_mult.shape[0] // 8
    G = parent_mult.shape[0] // 8
    n1, n2, n3 = fine.shape[1:4]
    m1, m2, m3 = parent.shape[1:4]
    masks = jnp.concatenate(
        [
            octant_grids(fine_mask.T, fine_bits).reshape(8, F, words),
            octant_grids(parent_mask.T, parent_bits).reshape(8, G, words),
        ],
        axis=1,
    )
    held = spread_masks(masks)
    for dim in (1, 2):
        fine, parent = exchange(fine, parent, dim, fine_bits, device_index, device_bits)
    is_odd = parity(0, fine_bits, device_index, device_bits)
    top = packed_face(fine, parent, 1, True)
    bottom = packed_face(fine, parent, 1, False)
    both = lax.all_gather(
        jnp.where(is_odd, top, bottom), "box", axis_index_groups=odd_groups(0, fine_bits, device_bits)
    )
    odd_got = jnp.where(is_odd, both[1], both[0])
    even_got = lax.ppermute(
        jnp.where(is_odd, bottom, top), "box", pair_route(0, 0, fine_bits, device_bits)
    )
    split = (n2 + 2) * (n3 + 2)

    def slab(got):
        return got[:, :split].reshape(8, 1, n2 + 2, n3 + 2, width)

    def parent_slab(got):
        return got[:, split:].reshape(8, 1, m2 + 2, m3 + 2, width)

    def across(block, w2, w3):
        return jnp.stack(
            [
                block[:, :, b : b + w2, c : c + w3].reshape(8, -1, width)
                for b in range(3)
                for c in range(3)
            ]
        )

    def moved_parents(got, goes_up):
        slab_got = parent_slab(got)
        up = jnp.concatenate([parent[:, 1:], slab_got], axis=1)
        down = jnp.concatenate([slab_got, parent[:, : m1 - 1]], axis=1)
        return across(jnp.where(goes_up, up, down), m2, m3)

    even = slab(even_got)
    x_even = across(jnp.concatenate([even, fine, even], axis=1), n2, n3)
    xp_even = jnp.concatenate(
        [across(parent, m2, m3), moved_parents(even_got, jnp.logical_not(is_odd))]
    ).reshape(-1, G, width)
    lists = shift_lists()
    slots = [126, 72]
    tables = []
    for odd in (False, True):
        near_side, far_side = (0, 2) if odd else (2, 0)
        tables.append(
            (
                work_table([lists[1], lists[near_side]], slots[0], n1 + 2, n2 * n3),
                work_table([lists[far_side]], slots[1], n1 + 2, n2 * n3),
            )
        )
    first_table = jnp.where(is_odd, tables[1][0], tables[0][0])
    last_table = jnp.where(is_odd, tables[1][1], tables[0][1])
    sums = first_terms(first_table, slots[0], held, x_even.reshape(-1, width), xp_even, kernels)
    odd_across = across(slab(odd_got), n2, n3)
    slab_rows = n2 * n3
    x_odd = lax.dynamic_update_slice(x_even, odd_across, (0, 0, 0, 0))
    x_odd = lax.dynamic_update_slice(x_odd, odd_across, (0, 0, (n1 + 1) * slab_rows, 0))
    xp_odd = moved_parents(odd_got, is_odd).reshape(-1, G, width)
    fine_local, parent_local = last_terms(
        last_table,
        slots[1],
        held,
        x_odd.reshape(-1, width),
        xp_odd,
        kernels,
        sums,
        shift_ops,
        jnp.asarray(parent_order(parent_bits), jnp.bfloat16),
    )
    fine_local = from_octants(fine_local, fine_bits)
    parent_local = from_octants(parent_local.reshape(8, G, width), parent_bits)
    return fine_local, parent_local


def from_octants(blocks, total_bits):
    width = blocks.shape[-1]
    bits = total_bits - 3
    axes_order, _ = grid_order(bits)
    grid = blocks.reshape((8,) + (2,) * bits + (width,))
    inverse = [0] * bits
    for position, source in enumerate(axes_order):
        inverse[source] = position
    moved = jnp.transpose(grid, tuple(1 + v for v in inverse) + (0, bits + 1))
    return moved.reshape(2**total_bits, width)


def solution(mesh):
    return jax.shard_map(
        on_device,
        mesh=mesh,
        in_specs=(P("box", None), P("box", None), P(None, "box"), P(None, "box"), P(), P()),
        out_specs=(P("box", None), P("box", None)),
        check_vma=False,
    )
```

```python
import jax
import jax.numpy as jnp
import numpy as np
from jax import lax
from jax.experimental import pallas as pl
from jax.experimental.pallas import tpu as pltpu
from jax.sharding import PartitionSpec as P

DIM_OF_BIT = (2, 1, 0)


def direction_table():
    listing = []
    picks = ([-2, -1, 0, 1, 2], [-3], [3])
    for ga in range(3):
        for gb in range(3):
            for gc in range(3):
                for oa in picks[ga]:
                    for ob in picks[gb]:
                        for oc in picks[gc]:
                            if max(abs(oa), abs(ob), abs(oc)) >= 2:
                                listing.append((oa, ob, oc, ga, gb, gc))
    return np.array(listing, np.int32)


def grid_order(total_bits):
    axes_order = []
    extents = []
    for target in range(3):
        chosen = [k for k in range(total_bits - 1, -1, -1) if 2 - k % 3 == target]
        axes_order += [total_bits - 1 - k for k in chosen]
        extents.append(2 ** len(chosen))
    return axes_order, extents


def to_grid(rows, total_bits):
    axes_order, extents = grid_order(total_bits)
    trailing = rows.shape[1:]
    bitwise = rows.reshape((2,) * total_bits + trailing)
    extra = tuple(range(total_bits, total_bits + len(trailing)))
    return jnp.transpose(bitwise, tuple(axes_order) + extra).reshape(tuple(extents) + trailing)


def grid_permutation(total_bits):
    axes_order, _ = grid_order(total_bits)
    numbers = np.arange(2**total_bits).reshape((2,) * total_bits)
    return np.transpose(numbers, axes_order).reshape(-1)


def octant_grids(rows, total_bits):
    width = rows.shape[1]
    parents = to_grid(rows.reshape(-1, 8, width), total_bits - 3)
    return jnp.moveaxis(parents, 3, 0)


def owned_bits(dim, low_bits, device_bits):
    return [k for k in range(device_bits) if 2 - (low_bits + k) % 3 == dim]


def pair_route(dim, odd, low_bits, device_bits):
    bits = owned_bits(dim, low_bits, device_bits)
    route = []
    for number in range(2**device_bits):
        place = sum(((number >> bit) & 1) << k for k, bit in enumerate(bits))
        other = place + (1 if place % 2 == odd else -1)
        if 0 <= other < 2 ** len(bits):
            target = number
            for k, bit in enumerate(bits):
                target = target & ~(1 << bit) | ((other >> k) & 1) << bit
            route.append((number, target))
    return route


def face(block, axis, last):
    at = block.shape[axis] - 1 if last else 0
    return lax.index_in_dim(block, at, axis, keepdims=False)


def packed_face(fine, parent, axis, last):
    pieces = [face(b, axis, last).reshape(8, -1, b.shape[-1]) for b in (fine, parent)]
    return jnp.concatenate(pieces, axis=1)


def parity(dim, low_bits, device_index, device_bits):
    first_bit = owned_bits(dim, low_bits, device_bits)[0]
    return (jnp.right_shift(device_index, first_bit) & 1) == 1


def exchange(fine, parent, dim, low_bits, device_index, device_bits):
    is_odd = parity(dim, low_bits, device_index, device_bits)
    axis = dim + 1
    top = packed_face(fine, parent, axis, True)
    bottom = packed_face(fine, parent, axis, False)
    even_send = jnp.where(is_odd, bottom, top)
    odd_send = jnp.where(is_odd, top, bottom)
    odd_got = lax.ppermute(odd_send, "box", pair_route(dim, 1, low_bits, device_bits))
    even_got = lax.ppermute(even_send, "box", pair_route(dim, 0, low_bits, device_bits))
    below = jnp.where(is_odd, even_got, odd_got)
    above = jnp.where(is_odd, odd_got, even_got)
    split = face(fine, axis, True).size // (8 * fine.shape[-1])
    out = []
    for block, pick in ((fine, slice(0, split)), (parent, slice(split, None))):
        shape = face(block, axis, True).shape
        low = jnp.expand_dims(below[:, pick].reshape(shape), axis)
        high = jnp.expand_dims(above[:, pick].reshape(shape), axis)
        out.append(jnp.concatenate([low, block, high], axis=axis))
    return out


def shift_lists():
    offsets = direction_table()
    lists = [[[] for _ in range(8)] for _ in range(3)]
    for octant in range(8):
        own = np.array([octant >> 2 & 1, octant >> 1 & 1, octant & 1])
        for number in range(offsets.shape[0]):
            moved = offsets[number, :3] + own
            if moved.min() < -2 or moved.max() > 3:
                continue
            shift = (moved >> 1) + 1
            source = moved & 1
            lists[shift[0]][octant].append((number, shift, source[0] * 4 + source[1] * 2 + source[2]))
    return lists


CHUNK = 18


def work_table(groups, slots, slab_count, slab_rows):
    table = np.zeros((5, 8, slots), np.int32)
    table[3] = -1
    for octant in range(8):
        at = 0
        for place, per_octant in enumerate(groups):
            for number, shift, source in per_octant[octant]:
                across = shift[1] * 3 + shift[2]
                table[0, octant, at] = number
                table[1, octant, at] = (across * 8 + source) * slab_count * slab_rows + shift[0] * slab_rows
                table[2, octant, at] = (place * 9 + across) * 8 + source
                table[3, octant, at] = number // 8
                table[4, octant, at] = number % 8
                at += 1
    return table


def unpack_masks(packed, byte_of, shift_of):
    octants, rows, count = packed.shape
    chunks = byte_of.shape[0]

    def kernel(packed, byte_of, shift_of, out):
        def one(octant, carry):
            lines = lax.broadcasted_iota(jnp.int32, (count, 128), 0)
            for c in range(chunks):
                pick = (lines == byte_of[c, pl.ds(octant, 1), :]).astype(jnp.float32).astype(jnp.bfloat16)
                value = jnp.dot(packed[octant], pick, preferred_element_type=jnp.float32).astype(jnp.int32)
                bit = jnp.right_shift(value, jnp.broadcast_to(shift_of[c, pl.ds(octant, 1), :], value.shape)) & 1
                out[c, octant] = bit.astype(jnp.float32)
            return carry

        lax.fori_loop(0, octants, one, 0)

    vmem = pl.BlockSpec(memory_space=pltpu.VMEM)
    return pl.pallas_call(
        kernel,
        out_shape=jax.ShapeDtypeStruct((chunks, octants, rows, 128), jnp.float32),
        in_specs=[vmem] * 3,
        out_specs=vmem,
        compiler_params=pltpu.CompilerParams(vmem_limit_bytes=16 << 20),
        name="unpack",
    )(packed, byte_of, shift_of)


def add_terms(table, slots, first, masks, x, xp, kernels, acc):
    F = acc.shape[1] - xp.shape[1]
    rows = acc.shape[1]

    def masked(place, column):
        row = pl.multiple_of(table[1, place], 16)
        value = jnp.concatenate([x[pl.ds(row, F), :], xp[table[2, place]]], axis=0)
        return value * jnp.broadcast_to(column, (rows, 128)).astype(jnp.bfloat16)

    def step(number, carry):
        at = number * CHUNK
        for octant in range(8):
            place = octant * slots + at
            columns = masks[first + number, octant]
            left = jnp.concatenate([masked(place + j, columns[:, j : j + 1]) for j in range(CHUNK)], axis=1)
            right = jnp.concatenate([kernels[table[0, place + j]] for j in range(CHUNK)], axis=0)
            acc[octant] += jnp.dot(left, right, preferred_element_type=jnp.float32)
        return carry

    lax.fori_loop(0, slots // CHUNK, step, 0)


def first_terms(table, slots, masks, x, xp, kernels):
    rows = masks.shape[2]
    width = kernels.shape[1]

    def kernel(table, masks, x, xp, kernels, acc):
        acc[...] = jnp.zeros_like(acc)
        add_terms(table, slots, 0, masks, x, xp, kernels, acc)

    vmem = pl.BlockSpec(memory_space=pltpu.VMEM)
    return pl.pallas_call(
        kernel,
        out_shape=jax.ShapeDtypeStruct((8, rows, width), jnp.float32),
        in_specs=[pl.BlockSpec(memory_space=pltpu.SMEM)] + [vmem] * 4,
        out_specs=vmem,
        compiler_params=pltpu.CompilerParams(vmem_limit_bytes=16 << 20),
        cost_estimate=pl.CostEstimate(
            flops=2 * 8 * rows * slots * width * width, transcendentals=0, bytes_accessed=x.size * 2
        ),
        name="first_terms",
    )(table, masks, x, xp, kernels)


def last_terms(table, slots, first, masks, x, xp, kernels, sums, shift_ops, perm):
    rows = masks.shape[2]
    width = kernels.shape[1]
    F = perm.shape[0]

    def kernel(table, masks, x, xp, kernels, sums, shift, perm, fine_out, parent_out, acc):
        acc[...] = sums[...]
        add_terms(table, slots, first, masks, x, xp, kernels, acc)
        far = [(acc[p, F:, :] * 0.5).astype(jnp.bfloat16) for p in range(8)]
        local = jnp.concatenate(far, axis=0)
        parent_out[...] = local
        ordered = jnp.dot(perm[...], local, preferred_element_type=jnp.float32).astype(jnp.bfloat16)
        for p in range(8):
            moved = jnp.dot(ordered, shift[p], preferred_element_type=jnp.float32)
            fine_out[p] = (acc[p, :F, :] + moved).astype(jnp.bfloat16)

    vmem = pl.BlockSpec(memory_space=pltpu.VMEM)
    return pl.pallas_call(
        kernel,
        out_shape=(
            jax.ShapeDtypeStruct((8, F, width), jnp.bfloat16),
            jax.ShapeDtypeStruct((8 * (rows - F), width), jnp.bfloat16),
        ),
        in_specs=[pl.BlockSpec(memory_space=pltpu.SMEM)] + [vmem] * 7,
        out_specs=(vmem, vmem),
        scratch_shapes=[pltpu.VMEM((8, rows, width), jnp.float32)],
        compiler_params=pltpu.CompilerParams(vmem_limit_bytes=16 << 20),
        name="last_terms",
    )(table, masks, x, xp, kernels, sums, shift_ops, perm)


def parent_order(parent_bits):
    count = 2**parent_bits
    held = np.arange(count).reshape(-1, 8)[grid_permutation(parent_bits - 3)].T.reshape(-1)
    place = np.zeros(count, np.int64)
    place[held] = np.arange(count)
    perm = np.zeros((count, count), np.float32)
    perm[np.arange(count), place[grid_permutation(parent_bits)]] = 1
    return perm


def on_device(fine_mult, parent_mult, fine_mask, parent_mask, kernels, shift_ops):
    device_bits = lax.axis_size("box").bit_length() - 1
    device_index = lax.axis_index("box")
    fine_bits = fine_mult.shape[0].bit_length() - 1
    parent_bits = parent_mult.shape[0].bit_length() - 1
    width = fine_mult.shape[1]
    words = fine_mask.shape[0]
    fine = octant_grids(fine_mult, fine_bits)
    parent = octant_grids(parent_mult, parent_bits)
    F = fine_mult.shape[0] // 8
    G = parent_mult.shape[0] // 8
    n1, n2, n3 = fine.shape[1:4]
    m1, m2, m3 = parent.shape[1:4]
    masks = jnp.concatenate(
        [
            octant_grids(fine_mask.T, fine_bits).reshape(8, F, words),
            octant_grids(parent_mask.T, parent_bits).reshape(8, G, words),
        ],
        axis=1,
    )
    is_odd = parity(0, fine_bits, device_index, device_bits)
    lists = shift_lists()
    slots = [126, 72]
    tables = []
    for odd in (False, True):
        near_side, far_side = (0, 2) if odd else (2, 0)
        tables.append(
            (
                work_table([lists[1], lists[near_side]], slots[0], n1 + 2, n2 * n3),
                work_table([lists[far_side]], slots[1], n1 + 2, n2 * n3),
            )
        )

    def by_parity(make):
        return jnp.where(is_odd, make(tables[1]), make(tables[0]))

    def columns(line):
        def make(pair):
            joined = np.concatenate([pair[0][line], pair[1][line]], axis=1)
            chunked = joined.reshape(8, -1, CHUNK).transpose(1, 0, 2)
            return np.pad(chunked, ((0, 0), (0, 0), (0, 128 - CHUNK)))

        return by_parity(make)

    first_table = by_parity(lambda pair: pair[0][:3].reshape(3, -1))
    last_table = by_parity(lambda pair: pair[1][:3].reshape(3, -1))
    packed = jnp.stack([masks & 255, jnp.right_shift(masks, 8)], axis=3).astype(jnp.bfloat16)
    held = unpack_masks(packed.reshape(8, F + G, 2 * words), columns(3), columns(4))
    for dim in (1, 2):
        fine, parent = exchange(fine, parent, dim, fine_bits, device_index, device_bits)
    top = packed_face(fine, parent, 1, True)
    bottom = packed_face(fine, parent, 1, False)
    even_got = lax.ppermute(
        jnp.where(is_odd, bottom, top), "box", pair_route(0, 0, fine_bits, device_bits)
    )
    odd_got = lax.ppermute(
        jnp.where(is_odd, top, bottom), "box", pair_route(0, 1, fine_bits, device_bits)
    )
    split = (n2 + 2) * (n3 + 2)

    def slab(got):
        return got[:, :split].reshape(8, 1, n2 + 2, n3 + 2, width)

    def parent_slab(got):
        return got[:, split:].reshape(8, 1, m2 + 2, m3 + 2, width)

    def across(block, w2, w3):
        return jnp.stack(
            [
                block[:, :, b : b + w2, c : c + w3].reshape(8, -1, width)
                for b in range(3)
                for c in range(3)
            ]
        )

    def moved_parents(got, goes_up):
        slab_got = parent_slab(got)
        up = jnp.concatenate([parent[:, 1:], slab_got], axis=1)
        down = jnp.concatenate([slab_got, parent[:, : m1 - 1]], axis=1)
        return across(jnp.where(goes_up, up, down), m2, m3)

    even = slab(even_got)
    x_even = across(jnp.concatenate([even, fine, even], axis=1), n2, n3)
    xp_even = jnp.concatenate(
        [across(parent, m2, m3), moved_parents(even_got, jnp.logical_not(is_odd))]
    ).reshape(-1, G, width)
    sums = first_terms(first_table, slots[0], held, x_even.reshape(-1, width), xp_even, kernels)
    sums, odd_got = lax.optimization_barrier((sums, odd_got))
    odd_across = across(slab(odd_got), n2, n3)
    slab_rows = n2 * n3
    x_odd = lax.dynamic_update_slice(x_even, odd_across, (0, 0, 0, 0))
    x_odd = lax.dynamic_update_slice(x_odd, odd_across, (0, 0, (n1 + 1) * slab_rows, 0))
    xp_odd = moved_parents(odd_got, is_odd).reshape(-1, G, width)
    fine_local, parent_local = last_terms(
        last_table,
        slots[1],
        slots[0] // CHUNK,
        held,
        x_odd.reshape(-1, width),
        xp_odd,
        kernels,
        sums,
        shift_ops,
        jnp.asarray(parent_order(parent_bits), jnp.bfloat16),
    )
    fine_local = from_octants(fine_local, fine_bits)
    parent_local = from_octants(parent_local.reshape(8, G, width), parent_bits)
    return fine_local, parent_local


def from_octants(blocks, total_bits):
    width = blocks.shape[-1]
    bits = total_bits - 3
    axes_order, _ = grid_order(bits)
    grid = blocks.reshape((8,) + (2,) * bits + (width,))
    inverse = [0] * bits
    for position, source in enumerate(axes_order):
        inverse[source] = position
    moved = jnp.transpose(grid, tuple(1 + v for v in inverse) + (0, bits + 1))
    return moved.reshape(2**total_bits, width)


def solution(mesh):
    return jax.shard_map(
        on_device,
        mesh=mesh,
        in_specs=(P("box", None), P("box", None), P(None, "box"), P(None, "box"), P(), P()),
        out_specs=(P("box", None), P("box", None)),
        check_vma=False,
    )
```

```python
import jax
import jax.numpy as jnp
import numpy as np
from jax import lax
from jax.experimental import pallas as pl
from jax.experimental.pallas import tpu as pltpu
from jax.sharding import PartitionSpec as P

DIM_OF_BIT = (2, 1, 0)


def direction_table():
    listing = []
    picks = ([-2, -1, 0, 1, 2], [-3], [3])
    for ga in range(3):
        for gb in range(3):
            for gc in range(3):
                for oa in picks[ga]:
                    for ob in picks[gb]:
                        for oc in picks[gc]:
                            if max(abs(oa), abs(ob), abs(oc)) >= 2:
                                listing.append((oa, ob, oc, ga, gb, gc))
    return np.array(listing, np.int32)


def grid_order(total_bits):
    axes_order = []
    extents = []
    for target in range(3):
        chosen = [k for k in range(total_bits - 1, -1, -1) if 2 - k % 3 == target]
        axes_order += [total_bits - 1 - k for k in chosen]
        extents.append(2 ** len(chosen))
    return axes_order, extents


def to_grid(rows, total_bits):
    axes_order, extents = grid_order(total_bits)
    trailing = rows.shape[1:]
    bitwise = rows.reshape((2,) * total_bits + trailing)
    extra = tuple(range(total_bits, total_bits + len(trailing)))
    return jnp.transpose(bitwise, tuple(axes_order) + extra).reshape(tuple(extents) + trailing)


def grid_permutation(total_bits):
    axes_order, _ = grid_order(total_bits)
    numbers = np.arange(2**total_bits).reshape((2,) * total_bits)
    return np.transpose(numbers, axes_order).reshape(-1)


def octant_grids(rows, total_bits):
    width = rows.shape[1]
    parents = to_grid(rows.reshape(-1, 8, width), total_bits - 3)
    return jnp.moveaxis(parents, 3, 0)


def owned_bits(dim, low_bits, device_bits):
    return [k for k in range(device_bits) if 2 - (low_bits + k) % 3 == dim]


def pair_route(dim, odd, low_bits, device_bits):
    bits = owned_bits(dim, low_bits, device_bits)
    route = []
    for number in range(2**device_bits):
        place = sum(((number >> bit) & 1) << k for k, bit in enumerate(bits))
        other = place + (1 if place % 2 == odd else -1)
        if 0 <= other < 2 ** len(bits):
            target = number
            for k, bit in enumerate(bits):
                target = target & ~(1 << bit) | ((other >> k) & 1) << bit
            route.append((number, target))
    return route


def face(block, axis, last):
    at = block.shape[axis] - 1 if last else 0
    return lax.index_in_dim(block, at, axis, keepdims=False)


def packed_face(fine, parent, axis, last):
    pieces = [face(b, axis, last).reshape(8, -1, b.shape[-1]) for b in (fine, parent)]
    return jnp.concatenate(pieces, axis=1)


def parity(dim, low_bits, device_index, device_bits):
    first_bit = owned_bits(dim, low_bits, device_bits)[0]
    return (jnp.right_shift(device_index, first_bit) & 1) == 1


def exchange(fine, parent, dim, low_bits, device_index, device_bits):
    is_odd = parity(dim, low_bits, device_index, device_bits)
    axis = dim + 1
    top = packed_face(fine, parent, axis, True)
    bottom = packed_face(fine, parent, axis, False)
    even_send = jnp.where(is_odd, bottom, top)
    odd_send = jnp.where(is_odd, top, bottom)
    odd_got = lax.ppermute(odd_send, "box", pair_route(dim, 1, low_bits, device_bits))
    even_got = lax.ppermute(even_send, "box", pair_route(dim, 0, low_bits, device_bits))
    below = jnp.where(is_odd, even_got, odd_got)
    above = jnp.where(is_odd, odd_got, even_got)
    split = face(fine, axis, True).size // (8 * fine.shape[-1])
    out = []
    for block, pick in ((fine, slice(0, split)), (parent, slice(split, None))):
        shape = face(block, axis, True).shape
        low = jnp.expand_dims(below[:, pick].reshape(shape), axis)
        high = jnp.expand_dims(above[:, pick].reshape(shape), axis)
        out.append(jnp.concatenate([low, block, high], axis=axis))
    return out


def shift_lists():
    offsets = direction_table()
    lists = [[[] for _ in range(8)] for _ in range(3)]
    for octant in range(8):
        own = np.array([octant >> 2 & 1, octant >> 1 & 1, octant & 1])
        for number in range(offsets.shape[0]):
            moved = offsets[number, :3] + own
            if moved.min() < -2 or moved.max() > 3:
                continue
            shift = (moved >> 1) + 1
            source = moved & 1
            lists[shift[0]][octant].append((number, shift, source[0] * 4 + source[1] * 2 + source[2]))
    return lists


CHUNK = 18
SHORTER = 9


def work_table(groups, slots, slab_count):
    table = np.zeros((3, 8, slots), np.int32)
    table[1] = -1
    for octant in range(8):
        at = 0
        for place, per_octant in enumerate(groups):
            for number, shift, source in per_octant[octant]:
                across = shift[1] * 3 + shift[2]
                row = (across * 8 + source) * slab_count + shift[0]
                table[0, octant, at] = number | row << 9 | ((place * 9 + across) * 8 + source) << 18
                table[1, octant, at] = number // 8
                table[2, octant, at] = number % 8
                at += 1
    return table


def unpack_masks(packed, byte_of, shift_of):
    octants, rows, count = packed.shape
    lanes = byte_of.shape[1]

    def kernel(packed, byte_of, shift_of, out):
        lines = lax.broadcasted_iota(jnp.int32, (count, lanes), 0)
        for octant in range(octants):
            pick = (lines == byte_of[octant : octant + 1, :]).astype(jnp.float32).astype(jnp.bfloat16)
            value = jnp.dot(packed[octant], pick, preferred_element_type=jnp.float32).astype(jnp.int32)
            amount = jnp.broadcast_to(shift_of[octant : octant + 1, :], value.shape)
            out[octant] = (jnp.right_shift(value, amount) & 1).astype(jnp.float32)

    vmem = pl.BlockSpec(memory_space=pltpu.VMEM)
    return pl.pallas_call(
        kernel,
        out_shape=jax.ShapeDtypeStruct((octants, rows, lanes), jnp.float32),
        in_specs=[vmem] * 3,
        out_specs=vmem,
        compiler_params=pltpu.CompilerParams(vmem_limit_bytes=16 << 20),
        name="unpack",
    )(packed, byte_of, shift_of)


def add_terms(table, slots, first, slab_rows, masks, x, xp, kernels, acc):
    F = acc.shape[1] - xp.shape[1]
    rows = acc.shape[1]

    def masked(place, column):
        entry = table[place]
        row = pl.multiple_of((jnp.right_shift(entry, 9) & 511) * slab_rows, 16)
        value = jnp.concatenate([x[pl.ds(row, F), :], xp[jnp.right_shift(entry, 18)]], axis=0)
        return value * jnp.broadcast_to(column, (rows, 128)).astype(jnp.bfloat16)

    longer = table[8 * slots]

    def run(lead, count):
        def one(number, carry):
            octant = lead + number
            columns = masks[octant]
            for at in range(0, count, CHUNK):
                part = range(at, min(at + CHUNK, count))
                place = octant * slots
                left = jnp.concatenate(
                    [masked(place + j, columns[:, first + j : first + j + 1]) for j in part], axis=1
                )
                right = jnp.concatenate([kernels[table[place + j] & 511] for j in part], axis=0)
                acc[octant] += jnp.dot(left, right, preferred_element_type=jnp.float32)
            return carry

        lax.fori_loop(0, 4, one, 0)

    run(longer, slots)
    run(4 - longer, slots - SHORTER)


def first_terms(table, slots, slab_rows, masks, x, xp, kernels):
    rows = masks.shape[1]
    width = kernels.shape[1]

    def kernel(table, masks, x, xp, kernels, acc):
        acc[...] = jnp.zeros_like(acc)
        add_terms(table, slots, 0, slab_rows, masks, x, xp, kernels, acc)

    vmem = pl.BlockSpec(memory_space=pltpu.VMEM)
    return pl.pallas_call(
        kernel,
        out_shape=jax.ShapeDtypeStruct((8, rows, width), jnp.float32),
        in_specs=[pl.BlockSpec(memory_space=pltpu.SMEM)] + [vmem] * 4,
        out_specs=vmem,
        compiler_params=pltpu.CompilerParams(vmem_limit_bytes=16 << 20),
        cost_estimate=pl.CostEstimate(
            flops=2 * 8 * rows * slots * width * width, transcendentals=0, bytes_accessed=x.size * 2
        ),
        name="first_terms",
    )(table, masks, x, xp, kernels)


def moved_rows(order, rows):
    return jnp.dot(order, rows, preferred_element_type=jnp.float32).astype(jnp.bfloat16)


def last_terms(table, slots, first, slab_rows, masks, x, xp, kernels, sums, shift_ops, perm, fine_back, parent_back):
    rows = masks.shape[1]
    width = kernels.shape[1]
    F = perm.shape[0]

    def kernel(table, masks, x, xp, kernels, sums, *refs):
        late, (fine_out, parent_out, acc, shift, perm, fine_back, parent_back, sems) = refs[:4], refs[4:]
        loads = []
        for number, (source, target) in enumerate(zip(late, (shift, perm, fine_back, parent_back))):
            load = pltpu.make_async_copy(source, target, sems.at[number])
            load.start()
            loads.append(load)
        acc[...] = sums[...]
        add_terms(table, slots, first, slab_rows, masks, x, xp, kernels, acc)
        for load in loads:
            load.wait()
        far = [(acc[p, F:, :] * 0.5).astype(jnp.bfloat16) for p in range(8)]
        local = jnp.concatenate(far, axis=0)
        parent_out[...] = moved_rows(parent_back[...], local)
        ordered = moved_rows(perm[...], local)
        near = []
        for p in range(8):
            moved = jnp.dot(ordered, shift[p], preferred_element_type=jnp.float32)
            near.append((acc[p, :F, :] + moved).astype(jnp.bfloat16))
        fine_out[...] = moved_rows(fine_back[...], jnp.concatenate(near, axis=0))

    vmem = pl.BlockSpec(memory_space=pltpu.VMEM)
    return pl.pallas_call(
        kernel,
        out_shape=(
            jax.ShapeDtypeStruct((8 * F, width), jnp.bfloat16),
            jax.ShapeDtypeStruct((8 * (rows - F), width), jnp.bfloat16),
        ),
        in_specs=[pl.BlockSpec(memory_space=pltpu.SMEM)] + [vmem] * 5 + [pl.BlockSpec(memory_space=pltpu.HBM)] * 4,
        out_specs=(vmem, vmem),
        scratch_shapes=[pltpu.VMEM((8, rows, width), jnp.float32)]
        + [pltpu.VMEM(v.shape, v.dtype) for v in (shift_ops, perm, fine_back, parent_back)]
        + [pltpu.SemaphoreType.DMA((4,))],
        compiler_params=pltpu.CompilerParams(vmem_limit_bytes=16 << 20),
        name="last_terms",
    )(table, masks, x, xp, kernels, sums, shift_ops, perm, fine_back, parent_back)


def parent_order(parent_bits):
    count = 2**parent_bits
    held = np.arange(count).reshape(-1, 8)[grid_permutation(parent_bits - 3)].T.reshape(-1)
    place = np.zeros(count, np.int64)
    place[held] = np.arange(count)
    perm = np.zeros((count, count), np.float32)
    perm[np.arange(count), place[grid_permutation(parent_bits)]] = 1
    return perm


def back_order(total_bits):
    count = 2**total_bits
    numbers = np.arange(count).reshape(-1, 8)[grid_permutation(total_bits - 3)].T.reshape(-1)
    order = np.zeros((count, count), np.float32)
    order[numbers, np.arange(count)] = 1
    return order


def on_device(fine_mult, parent_mult, fine_mask, parent_mask, kernels, shift_ops):
    device_bits = lax.axis_size("box").bit_length() - 1
    device_index = lax.axis_index("box")
    fine_bits = fine_mult.shape[0].bit_length() - 1
    parent_bits = parent_mult.shape[0].bit_length() - 1
    width = fine_mult.shape[1]
    words = fine_mask.shape[0]
    fine = octant_grids(fine_mult, fine_bits)
    parent = octant_grids(parent_mult, parent_bits)
    F = fine_mult.shape[0] // 8
    G = parent_mult.shape[0] // 8
    n1, n2, n3 = fine.shape[1:4]
    m1, m2, m3 = parent.shape[1:4]
    is_odd = parity(0, fine_bits, device_index, device_bits)
    lists = shift_lists()
    slots = [126, 72]
    tables = []
    for odd in (False, True):
        near_side, far_side = (0, 2) if odd else (2, 0)
        tables.append(
            (
                work_table([lists[1], lists[near_side]], slots[0], n1 + 2),
                work_table([lists[far_side]], slots[1], n1 + 2),
            )
        )

    def by_parity(make):
        return jnp.where(is_odd, make(tables[1]), make(tables[0]))

    def columns(line):
        def make(pair):
            joined = np.concatenate([pair[0][line], pair[1][line]], axis=1)
            return np.pad(joined, ((0, 0), (0, -joined.shape[1] % 128)))

        return by_parity(make)

    def entries(which):
        def make(pair):
            lengths = (pair[which][1] >= 0).sum(axis=1)
            lead = 0 if lengths[0] > lengths[4] else 4
            assert set(lengths[lead : lead + 4]) == {slots[which]}
            assert set(lengths[4 - lead : 8 - lead]) == {slots[which] - SHORTER}
            return np.concatenate([pair[which][0].reshape(-1), np.array([lead], np.int32)])

        return by_parity(make)

    first_table = entries(0)
    last_table = entries(1)
    fine, parent = exchange(fine, parent, 1, fine_bits, device_index, device_bits)
    fine, parent, fine_mask, parent_mask = lax.optimization_barrier(
        (fine, parent, fine_mask, parent_mask)
    )
    masks = jnp.concatenate(
        [
            octant_grids(fine_mask.T, fine_bits).reshape(8, F, words),
            octant_grids(parent_mask.T, parent_bits).reshape(8, G, words),
        ],
        axis=1,
    )
    packed = jnp.stack([masks & 255, jnp.right_shift(masks, 8)], axis=3).astype(jnp.bfloat16)
    held = unpack_masks(packed.reshape(8, F + G, 2 * words), columns(1), columns(2))
    fine, parent = exchange(fine, parent, 2, fine_bits, device_index, device_bits)
    top = packed_face(fine, parent, 1, True)
    bottom = packed_face(fine, parent, 1, False)
    even_got = lax.ppermute(
        jnp.where(is_odd, bottom, top), "box", pair_route(0, 0, fine_bits, device_bits)
    )
    odd_got = lax.ppermute(
        jnp.where(is_odd, top, bottom), "box", pair_route(0, 1, fine_bits, device_bits)
    )
    split = (n2 + 2) * (n3 + 2)

    def slab(got):
        return got[:, :split].reshape(8, 1, n2 + 2, n3 + 2, width)

    def parent_slab(got):
        return got[:, split:].reshape(8, 1, m2 + 2, m3 + 2, width)

    def across(block, w2, w3):
        return jnp.stack(
            [
                block[:, :, b : b + w2, c : c + w3].reshape(8, -1, width)
                for b in range(3)
                for c in range(3)
            ]
        )

    def moved_parents(got, goes_up):
        slab_got = parent_slab(got)
        up = jnp.concatenate([parent[:, 1:], slab_got], axis=1)
        down = jnp.concatenate([slab_got, parent[:, : m1 - 1]], axis=1)
        return across(jnp.where(goes_up, up, down), m2, m3)

    even = slab(even_got)
    x_even = across(jnp.concatenate([even, fine, even], axis=1), n2, n3)
    xp_even = jnp.concatenate(
        [across(parent, m2, m3), moved_parents(even_got, jnp.logical_not(is_odd))]
    ).reshape(-1, G, width)
    sums = first_terms(first_table, slots[0], n2 * n3, held, x_even.reshape(-1, width), xp_even, kernels)
    sums, odd_got = lax.optimization_barrier((sums, odd_got))
    odd_across = across(slab(odd_got), n2, n3)
    slab_rows = n2 * n3
    x_odd = lax.dynamic_update_slice(x_even, odd_across, (0, 0, 0, 0))
    x_odd = lax.dynamic_update_slice(x_odd, odd_across, (0, 0, (n1 + 1) * slab_rows, 0))
    xp_odd = moved_parents(odd_got, is_odd).reshape(-1, G, width)
    fine_local, parent_local = last_terms(
        last_table,
        slots[1],
        slots[0],
        n2 * n3,
        held,
        x_odd.reshape(-1, width),
        xp_odd,
        kernels,
        sums,
        shift_ops,
        jnp.asarray(parent_order(parent_bits), jnp.bfloat16),
        jnp.asarray(back_order(fine_bits), jnp.bfloat16),
        jnp.asarray(back_order(parent_bits), jnp.bfloat16),
    )
    return fine_local, parent_local


def solution(mesh):
    return jax.shard_map(
        on_device,
        mesh=mesh,
        in_specs=(P("box", None), P("box", None), P(None, "box"), P(None, "box"), P(), P()),
        out_specs=(P("box", None), P("box", None)),
        check_vma=False,
    )
```

```python
import jax
import jax.numpy as jnp
import numpy as np
from jax import lax
from jax.experimental import pallas as pl
from jax.experimental.pallas import tpu as pltpu
from jax.sharding import PartitionSpec as P

DIM_OF_BIT = (2, 1, 0)


def direction_table():
    listing = []
    picks = ([-2, -1, 0, 1, 2], [-3], [3])
    for ga in range(3):
        for gb in range(3):
            for gc in range(3):
                for oa in picks[ga]:
                    for ob in picks[gb]:
                        for oc in picks[gc]:
                            if max(abs(oa), abs(ob), abs(oc)) >= 2:
                                listing.append((oa, ob, oc, ga, gb, gc))
    return np.array(listing, np.int32)


def grid_order(total_bits):
    axes_order = []
    extents = []
    for target in range(3):
        chosen = [k for k in range(total_bits - 1, -1, -1) if 2 - k % 3 == target]
        axes_order += [total_bits - 1 - k for k in chosen]
        extents.append(2 ** len(chosen))
    return axes_order, extents


def to_grid(rows, total_bits):
    axes_order, extents = grid_order(total_bits)
    trailing = rows.shape[1:]
    bitwise = rows.reshape((2,) * total_bits + trailing)
    extra = tuple(range(total_bits, total_bits + len(trailing)))
    return jnp.transpose(bitwise, tuple(axes_order) + extra).reshape(tuple(extents) + trailing)


def grid_permutation(total_bits):
    axes_order, _ = grid_order(total_bits)
    numbers = np.arange(2**total_bits).reshape((2,) * total_bits)
    return np.transpose(numbers, axes_order).reshape(-1)


def octant_grids(rows, total_bits):
    width = rows.shape[1]
    parents = to_grid(rows.reshape(-1, 8, width), total_bits - 3)
    return jnp.moveaxis(parents, 3, 0)


def owned_bits(dim, low_bits, device_bits):
    return [k for k in range(device_bits) if 2 - (low_bits + k) % 3 == dim]


def pair_route(dim, odd, low_bits, device_bits):
    bits = owned_bits(dim, low_bits, device_bits)
    route = []
    for number in range(2**device_bits):
        place = sum(((number >> bit) & 1) << k for k, bit in enumerate(bits))
        other = place + (1 if place % 2 == odd else -1)
        if 0 <= other < 2 ** len(bits):
            target = number
            for k, bit in enumerate(bits):
                target = target & ~(1 << bit) | ((other >> k) & 1) << bit
            route.append((number, target))
    return route


def face(block, axis, last):
    at = block.shape[axis] - 1 if last else 0
    return lax.index_in_dim(block, at, axis, keepdims=False)


def packed_face(fine, parent, axis, last):
    pieces = [face(b, axis, last).reshape(8, -1, b.shape[-1]) for b in (fine, parent)]
    return jnp.concatenate(pieces, axis=1)


def parity(dim, low_bits, device_index, device_bits):
    first_bit = owned_bits(dim, low_bits, device_bits)[0]
    return (jnp.right_shift(device_index, first_bit) & 1) == 1


def exchange(fine, parent, dim, low_bits, device_index, device_bits):
    is_odd = parity(dim, low_bits, device_index, device_bits)
    axis = dim + 1
    top = packed_face(fine, parent, axis, True)
    bottom = packed_face(fine, parent, axis, False)
    even_send = jnp.where(is_odd, bottom, top)
    odd_send = jnp.where(is_odd, top, bottom)
    odd_got = lax.ppermute(odd_send, "box", pair_route(dim, 1, low_bits, device_bits))
    even_got = lax.ppermute(even_send, "box", pair_route(dim, 0, low_bits, device_bits))
    below = jnp.where(is_odd, even_got, odd_got)
    above = jnp.where(is_odd, odd_got, even_got)
    split = face(fine, axis, True).size // (8 * fine.shape[-1])
    out = []
    for block, pick in ((fine, slice(0, split)), (parent, slice(split, None))):
        shape = face(block, axis, True).shape
        low = jnp.expand_dims(below[:, pick].reshape(shape), axis)
        high = jnp.expand_dims(above[:, pick].reshape(shape), axis)
        out.append(jnp.concatenate([low, block, high], axis=axis))
    return out


def shift_lists():
    offsets = direction_table()
    lists = [[[] for _ in range(8)] for _ in range(3)]
    for octant in range(8):
        own = np.array([octant >> 2 & 1, octant >> 1 & 1, octant & 1])
        for number in range(offsets.shape[0]):
            moved = offsets[number, :3] + own
            if moved.min() < -2 or moved.max() > 3:
                continue
            shift = (moved >> 1) + 1
            source = moved & 1
            lists[shift[0]][octant].append((number, shift, source[0] * 4 + source[1] * 2 + source[2]))
    return lists


CHUNK = 18
SHORTER = 9


def work_table(groups, slots, slab_count):
    table = np.zeros((3, 8, slots), np.int32)
    table[1] = -1
    for octant in range(8):
        at = 0
        for place, per_octant in enumerate(groups):
            for number, shift, source in per_octant[octant]:
                across = shift[1] * 3 + shift[2]
                row = (across * 8 + source) * slab_count + shift[0]
                table[0, octant, at] = number | row << 9 | ((place * 9 + across) * 8 + source) << 18
                table[1, octant, at] = number // 8
                table[2, octant, at] = number % 8
                at += 1
    return table


def unpack_masks(packed, byte_of, shift_of):
    octants, rows, count = packed.shape
    lanes = byte_of.shape[1]

    def kernel(packed, byte_of, shift_of, out):
        lines = lax.broadcasted_iota(jnp.int32, (count, lanes), 0)
        for octant in range(octants):
            pick = (lines == byte_of[octant : octant + 1, :]).astype(jnp.float32).astype(jnp.bfloat16)
            value = jnp.dot(packed[octant], pick, preferred_element_type=jnp.float32).astype(jnp.int32)
            amount = jnp.broadcast_to(shift_of[octant : octant + 1, :], value.shape)
            out[octant] = (jnp.right_shift(value, amount) & 1).astype(jnp.float32)

    vmem = pl.BlockSpec(memory_space=pltpu.VMEM)
    return pl.pallas_call(
        kernel,
        out_shape=jax.ShapeDtypeStruct((octants, rows, lanes), jnp.float32),
        in_specs=[vmem] * 3,
        out_specs=vmem,
        compiler_params=pltpu.CompilerParams(vmem_limit_bytes=16 << 20),
        name="unpack",
    )(packed, byte_of, shift_of)


def add_terms(table, slots, first, slab_rows, masks, x, xp, kernels, acc):
    F = acc.shape[1] - xp.shape[1]
    rows = acc.shape[1]

    def masked(place, column):
        entry = table[place]
        row = pl.multiple_of((jnp.right_shift(entry, 9) & 511) * slab_rows, 16)
        value = jnp.concatenate([x[pl.ds(row, F), :], xp[jnp.right_shift(entry, 18)]], axis=0)
        return value * jnp.broadcast_to(column, (rows, 128)).astype(jnp.bfloat16)

    longer = table[8 * slots]

    def run(lead, count):
        def one(number, carry):
            octant = lead + number
            columns = masks[octant]
            for at in range(0, count, CHUNK):
                part = range(at, min(at + CHUNK, count))
                place = octant * slots
                left = jnp.concatenate(
                    [masked(place + j, columns[:, first + j : first + j + 1]) for j in part], axis=1
                )
                right = jnp.concatenate([kernels[table[place + j] & 511] for j in part], axis=0)
                acc[octant] += jnp.dot(left, right, preferred_element_type=jnp.float32)
            return carry

        lax.fori_loop(0, 4, one, 0)

    run(longer, slots)
    run(4 - longer, slots - SHORTER)


def first_terms(table, slots, slab_rows, masks, x, xp, kernels):
    rows = masks.shape[1]
    width = kernels.shape[1]

    def kernel(table, masks, x, xp, kernels, acc):
        acc[...] = jnp.zeros_like(acc)
        add_terms(table, slots, 0, slab_rows, masks, x, xp, kernels, acc)

    vmem = pl.BlockSpec(memory_space=pltpu.VMEM)
    return pl.pallas_call(
        kernel,
        out_shape=jax.ShapeDtypeStruct((8, rows, width), jnp.float32),
        in_specs=[pl.BlockSpec(memory_space=pltpu.SMEM)] + [vmem] * 4,
        out_specs=vmem,
        compiler_params=pltpu.CompilerParams(vmem_limit_bytes=16 << 20),
        cost_estimate=pl.CostEstimate(
            flops=2 * 8 * rows * slots * width * width, transcendentals=0, bytes_accessed=x.size * 2
        ),
        name="first_terms",
    )(table, masks, x, xp, kernels)


def moved_rows(order, rows):
    return jnp.dot(order, rows, preferred_element_type=jnp.float32).astype(jnp.bfloat16)


def last_terms(table, slots, first, slab_rows, masks, x, xp, kernels, sums, shift_ops, perm, fine_back, parent_back):
    rows = masks.shape[1]
    width = kernels.shape[1]
    F = perm.shape[0]

    def kernel(
        table, masks, x, xp, kernels, sums, shift, perm, fine_back, parent_back, fine_out, parent_out, acc, rows_out
    ):
        acc[...] = sums[...]
        add_terms(table, slots, first, slab_rows, masks, x, xp, kernels, acc)
        far = [(acc[p, F:, :] * 0.5).astype(jnp.bfloat16) for p in range(8)]
        local = jnp.concatenate(far, axis=0)
        parent_out[...] = moved_rows(parent_back[...], local)
        ordered = moved_rows(perm[...], local)
        near = []
        for p in range(8):
            moved = jnp.dot(ordered, shift[p], preferred_element_type=jnp.float32)
            near.append((acc[p, :F, :] + moved).astype(jnp.bfloat16))
        whole = jnp.dot(fine_back[...], jnp.concatenate(near, axis=1), preferred_element_type=jnp.float32)
        for p in range(8):
            rows_out[:, p, :] = whole[:, p * width : (p + 1) * width]
        fine_out[...] = rows_out[...].reshape(8 * F, width).astype(jnp.bfloat16)

    vmem = pl.BlockSpec(memory_space=pltpu.VMEM)
    return pl.pallas_call(
        kernel,
        out_shape=(
            jax.ShapeDtypeStruct((8 * F, width), jnp.bfloat16),
            jax.ShapeDtypeStruct((8 * (rows - F), width), jnp.bfloat16),
        ),
        in_specs=[pl.BlockSpec(memory_space=pltpu.SMEM)] + [vmem] * 9,
        out_specs=(vmem, vmem),
        scratch_shapes=[pltpu.VMEM((8, rows, width), jnp.float32), pltpu.VMEM((F, 8, width), jnp.float32)],
        compiler_params=pltpu.CompilerParams(vmem_limit_bytes=16 << 20),
        name="last_terms",
    )(table, masks, x, xp, kernels, sums, shift_ops, perm, fine_back, parent_back)


def parent_order(parent_bits):
    count = 2**parent_bits
    held = np.arange(count).reshape(-1, 8)[grid_permutation(parent_bits - 3)].T.reshape(-1)
    place = np.zeros(count, np.int64)
    place[held] = np.arange(count)
    perm = np.zeros((count, count), np.float32)
    perm[np.arange(count), place[grid_permutation(parent_bits)]] = 1
    return perm


def grid_back(total_bits):
    order = np.zeros((2**total_bits, 2**total_bits), np.float32)
    order[grid_permutation(total_bits), np.arange(2**total_bits)] = 1
    return order


def back_order(total_bits):
    count = 2**total_bits
    numbers = np.arange(count).reshape(-1, 8)[grid_permutation(total_bits - 3)].T.reshape(-1)
    order = np.zeros((count, count), np.float32)
    order[numbers, np.arange(count)] = 1
    return order


def on_device(fine_mult, parent_mult, fine_mask, parent_mask, kernels, shift_ops):
    device_bits = lax.axis_size("box").bit_length() - 1
    device_index = lax.axis_index("box")
    fine_bits = fine_mult.shape[0].bit_length() - 1
    parent_bits = parent_mult.shape[0].bit_length() - 1
    width = fine_mult.shape[1]
    words = fine_mask.shape[0]
    fine = octant_grids(fine_mult, fine_bits)
    parent = octant_grids(parent_mult, parent_bits)
    F = fine_mult.shape[0] // 8
    G = parent_mult.shape[0] // 8
    n1, n2, n3 = fine.shape[1:4]
    m1, m2, m3 = parent.shape[1:4]
    is_odd = parity(0, fine_bits, device_index, device_bits)
    lists = shift_lists()
    slots = [126, 72]
    tables = []
    for odd in (False, True):
        near_side, far_side = (0, 2) if odd else (2, 0)
        tables.append(
            (
                work_table([lists[1], lists[near_side]], slots[0], n1 + 2),
                work_table([lists[far_side]], slots[1], n1 + 2),
            )
        )

    def by_parity(make):
        return jnp.where(is_odd, make(tables[1]), make(tables[0]))

    def columns(line):
        def make(pair):
            joined = np.concatenate([pair[0][line], pair[1][line]], axis=1)
            return np.pad(joined, ((0, 0), (0, -joined.shape[1] % 128)))

        return by_parity(make)

    def entries(which):
        def make(pair):
            lengths = (pair[which][1] >= 0).sum(axis=1)
            lead = 0 if lengths[0] > lengths[4] else 4
            assert set(lengths[lead : lead + 4]) == {slots[which]}
            assert set(lengths[4 - lead : 8 - lead]) == {slots[which] - SHORTER}
            return np.concatenate([pair[which][0].reshape(-1), np.array([lead], np.int32)])

        return by_parity(make)

    first_table = entries(0)
    last_table = entries(1)
    fine, parent = exchange(fine, parent, 1, fine_bits, device_index, device_bits)
    fine, parent, fine_mask, parent_mask = lax.optimization_barrier(
        (fine, parent, fine_mask, parent_mask)
    )
    masks = jnp.concatenate(
        [
            octant_grids(fine_mask.T, fine_bits).reshape(8, F, words),
            octant_grids(parent_mask.T, parent_bits).reshape(8, G, words),
        ],
        axis=1,
    )
    packed = jnp.stack([masks & 255, jnp.right_shift(masks, 8)], axis=3).astype(jnp.bfloat16)
    held = unpack_masks(packed.reshape(8, F + G, 2 * words), columns(1), columns(2))
    fine, parent = exchange(fine, parent, 2, fine_bits, device_index, device_bits)
    top = packed_face(fine, parent, 1, True)
    bottom = packed_face(fine, parent, 1, False)
    even_got = lax.ppermute(
        jnp.where(is_odd, bottom, top), "box", pair_route(0, 0, fine_bits, device_bits)
    )
    odd_got = lax.ppermute(
        jnp.where(is_odd, top, bottom), "box", pair_route(0, 1, fine_bits, device_bits)
    )
    split = (n2 + 2) * (n3 + 2)

    def slab(got):
        return got[:, :split].reshape(8, 1, n2 + 2, n3 + 2, width)

    def parent_slab(got):
        return got[:, split:].reshape(8, 1, m2 + 2, m3 + 2, width)

    def across(block, w2, w3):
        return jnp.stack(
            [
                block[:, :, b : b + w2, c : c + w3].reshape(8, -1, width)
                for b in range(3)
                for c in range(3)
            ]
        )

    def moved_parents(got, goes_up):
        slab_got = parent_slab(got)
        up = jnp.concatenate([parent[:, 1:], slab_got], axis=1)
        down = jnp.concatenate([slab_got, parent[:, : m1 - 1]], axis=1)
        return across(jnp.where(goes_up, up, down), m2, m3)

    even = slab(even_got)
    x_even = across(jnp.concatenate([even, fine, even], axis=1), n2, n3)
    xp_even = jnp.concatenate(
        [across(parent, m2, m3), moved_parents(even_got, jnp.logical_not(is_odd))]
    ).reshape(-1, G, width)
    sums = first_terms(first_table, slots[0], n2 * n3, held, x_even.reshape(-1, width), xp_even, kernels)
    sums, odd_got = lax.optimization_barrier((sums, odd_got))
    odd_across = across(slab(odd_got), n2, n3)
    slab_rows = n2 * n3
    x_odd = lax.dynamic_update_slice(x_even, odd_across, (0, 0, 0, 0))
    x_odd = lax.dynamic_update_slice(x_odd, odd_across, (0, 0, (n1 + 1) * slab_rows, 0))
    xp_odd = moved_parents(odd_got, is_odd).reshape(-1, G, width)
    fine_local, parent_local = last_terms(
        last_table,
        slots[1],
        slots[0],
        n2 * n3,
        held,
        x_odd.reshape(-1, width),
        xp_odd,
        kernels,
        sums,
        shift_ops,
        jnp.asarray(parent_order(parent_bits), jnp.bfloat16),
        jnp.asarray(grid_back(parent_bits), jnp.bfloat16),
        jnp.asarray(back_order(parent_bits), jnp.bfloat16),
    )
    return fine_local, parent_local


def solution(mesh):
    return jax.shard_map(
        on_device,
        mesh=mesh,
        in_specs=(P("box", None), P("box", None), P(None, "box"), P(None, "box"), P(), P()),
        out_specs=(P("box", None), P("box", None)),
        check_vma=False,
    )
```

```python
import jax
import jax.numpy as jnp
import numpy as np
from jax import lax
from jax.experimental import pallas as pl
from jax.experimental.pallas import tpu as pltpu
from jax.sharding import PartitionSpec as P

DIM_OF_BIT = (2, 1, 0)


def direction_table():
    listing = []
    picks = ([-2, -1, 0, 1, 2], [-3], [3])
    for ga in range(3):
        for gb in range(3):
            for gc in range(3):
                for oa in picks[ga]:
                    for ob in picks[gb]:
                        for oc in picks[gc]:
                            if max(abs(oa), abs(ob), abs(oc)) >= 2:
                                listing.append((oa, ob, oc, ga, gb, gc))
    return np.array(listing, np.int32)


def grid_order(total_bits):
    axes_order = []
    extents = []
    for target in range(3):
        chosen = [k for k in range(total_bits - 1, -1, -1) if 2 - k % 3 == target]
        axes_order += [total_bits - 1 - k for k in chosen]
        extents.append(2 ** len(chosen))
    return axes_order, extents


def to_grid(rows, total_bits):
    axes_order, extents = grid_order(total_bits)
    trailing = rows.shape[1:]
    bitwise = rows.reshape((2,) * total_bits + trailing)
    extra = tuple(range(total_bits, total_bits + len(trailing)))
    return jnp.transpose(bitwise, tuple(axes_order) + extra).reshape(tuple(extents) + trailing)


def grid_permutation(total_bits):
    axes_order, _ = grid_order(total_bits)
    numbers = np.arange(2**total_bits).reshape((2,) * total_bits)
    return np.transpose(numbers, axes_order).reshape(-1)


def octant_grids(rows, total_bits):
    width = rows.shape[1]
    parents = to_grid(rows.reshape(-1, 8, width), total_bits - 3)
    return jnp.moveaxis(parents, 3, 0)


def owned_bits(dim, low_bits, device_bits):
    return [k for k in range(device_bits) if 2 - (low_bits + k) % 3 == dim]


def pair_route(dim, odd, low_bits, device_bits):
    bits = owned_bits(dim, low_bits, device_bits)
    route = []
    for number in range(2**device_bits):
        place = sum(((number >> bit) & 1) << k for k, bit in enumerate(bits))
        other = place + (1 if place % 2 == odd else -1)
        if 0 <= other < 2 ** len(bits):
            target = number
            for k, bit in enumerate(bits):
                target = target & ~(1 << bit) | ((other >> k) & 1) << bit
            route.append((number, target))
    return route


def face(block, axis, last):
    at = block.shape[axis] - 1 if last else 0
    return lax.index_in_dim(block, at, axis, keepdims=False)


def packed_face(fine, parent, axis, last):
    pieces = [face(b, axis, last).reshape(8, -1, b.shape[-1]) for b in (fine, parent)]
    return jnp.concatenate(pieces, axis=1)


def parity(dim, low_bits, device_index, device_bits):
    first_bit = owned_bits(dim, low_bits, device_bits)[0]
    return (jnp.right_shift(device_index, first_bit) & 1) == 1


def exchange(fine, parent, dim, low_bits, device_index, device_bits):
    is_odd = parity(dim, low_bits, device_index, device_bits)
    axis = dim + 1
    top = packed_face(fine, parent, axis, True)
    bottom = packed_face(fine, parent, axis, False)
    even_send = jnp.where(is_odd, bottom, top)
    odd_send = jnp.where(is_odd, top, bottom)
    odd_got = lax.ppermute(odd_send, "box", pair_route(dim, 1, low_bits, device_bits))
    even_got = lax.ppermute(even_send, "box", pair_route(dim, 0, low_bits, device_bits))
    below = jnp.where(is_odd, even_got, odd_got)
    above = jnp.where(is_odd, odd_got, even_got)
    split = face(fine, axis, True).size // (8 * fine.shape[-1])
    out = []
    for block, pick in ((fine, slice(0, split)), (parent, slice(split, None))):
        shape = face(block, axis, True).shape
        low = jnp.expand_dims(below[:, pick].reshape(shape), axis)
        high = jnp.expand_dims(above[:, pick].reshape(shape), axis)
        out.append(jnp.concatenate([low, block, high], axis=axis))
    return out


def shift_lists():
    offsets = direction_table()
    lists = [[[] for _ in range(8)] for _ in range(3)]
    for octant in range(8):
        own = np.array([octant >> 2 & 1, octant >> 1 & 1, octant & 1])
        for number in range(offsets.shape[0]):
            moved = offsets[number, :3] + own
            if moved.min() < -2 or moved.max() > 3:
                continue
            shift = (moved >> 1) + 1
            source = moved & 1
            lists[shift[0]][octant].append((number, shift, source[0] * 4 + source[1] * 2 + source[2]))
    return lists


CHUNK = 18
SHORTER = 9


def work_table(groups, slots, slab_count):
    table = np.zeros((3, 8, slots), np.int32)
    table[1] = -1
    for octant in range(8):
        at = 0
        for place, per_octant in enumerate(groups):
            for number, shift, source in per_octant[octant]:
                across = shift[1] * 3 + shift[2]
                row = (across * 8 + source) * slab_count + shift[0]
                table[0, octant, at] = number | row << 9 | ((place * 9 + across) * 8 + source) << 18
                table[1, octant, at] = number // 8
                table[2, octant, at] = number % 8
                at += 1
    return table


def unpack_masks(packed, byte_of, shift_of):
    octants, rows, count = packed.shape
    lanes = byte_of.shape[1]

    def kernel(packed, byte_of, shift_of, out):
        lines = lax.broadcasted_iota(jnp.int32, (count, lanes), 0)
        for octant in range(octants):
            pick = (lines == byte_of[octant : octant + 1, :]).astype(jnp.float32).astype(jnp.bfloat16)
            value = jnp.dot(packed[octant], pick, preferred_element_type=jnp.float32).astype(jnp.int32)
            amount = jnp.broadcast_to(shift_of[octant : octant + 1, :], value.shape)
            out[octant] = (jnp.right_shift(value, amount) & 1).astype(jnp.float32)

    vmem = pl.BlockSpec(memory_space=pltpu.VMEM)
    return pl.pallas_call(
        kernel,
        out_shape=jax.ShapeDtypeStruct((octants, rows, lanes), jnp.float32),
        in_specs=[vmem] * 3,
        out_specs=vmem,
        compiler_params=pltpu.CompilerParams(vmem_limit_bytes=16 << 20),
        name="unpack",
    )(packed, byte_of, shift_of)


def add_terms(table, slots, first, slab_rows, masks, x, xp, kernels, acc):
    F = acc.shape[1] - xp.shape[1]
    rows = acc.shape[1]

    def spread_pair(one, two):
        code = jnp.broadcast_to(one + 2.0 * two, (rows, 128)).astype(jnp.bfloat16)
        high = jnp.clip(code - 1, 0, 1)
        return code - 2 * high, high

    def masked(place, spread):
        entry = table[place]
        row = pl.multiple_of((jnp.right_shift(entry, 9) & 511) * slab_rows, 16)
        value = jnp.concatenate([x[pl.ds(row, F), :], xp[jnp.right_shift(entry, 18)]], axis=0)
        return value * spread

    longer = table[8 * slots]

    def run(lead, count):
        def one(number, carry):
            octant = lead + number
            columns = masks[octant]
            for at in range(0, count, CHUNK):
                part = range(at, min(at + CHUNK, count))
                place = octant * slots
                spread = []
                for j in range(part.start, part.stop, 2):
                    at_j = first + j
                    spread += spread_pair(columns[:, at_j : at_j + 1], columns[:, at_j + 1 : at_j + 2])
                left = jnp.concatenate([masked(place + j, m) for j, m in zip(part, spread)], axis=1)
                right = jnp.concatenate([kernels[table[place + j] & 511] for j in part], axis=0)
                acc[octant] += jnp.dot(left, right, preferred_element_type=jnp.float32)
            return carry

        lax.fori_loop(0, 4, one, 0)

    run(longer, slots)
    run(4 - longer, slots - SHORTER)


def first_terms(table, slots, slab_rows, masks, x, xp, kernels):
    rows = masks.shape[1]
    width = kernels.shape[1]

    def kernel(table, masks, x, xp, kernels, acc):
        acc[...] = jnp.zeros_like(acc)
        add_terms(table, slots, 0, slab_rows, masks, x, xp, kernels, acc)

    vmem = pl.BlockSpec(memory_space=pltpu.VMEM)
    return pl.pallas_call(
        kernel,
        out_shape=jax.ShapeDtypeStruct((8, rows, width), jnp.float32),
        in_specs=[pl.BlockSpec(memory_space=pltpu.SMEM)] + [vmem] * 4,
        out_specs=vmem,
        compiler_params=pltpu.CompilerParams(vmem_limit_bytes=16 << 20),
        cost_estimate=pl.CostEstimate(
            flops=2 * 8 * rows * slots * width * width, transcendentals=0, bytes_accessed=x.size * 2
        ),
        name="first_terms",
    )(table, masks, x, xp, kernels)


def moved_rows(order, rows):
    return jnp.dot(order, rows, preferred_element_type=jnp.float32).astype(jnp.bfloat16)


def last_terms(table, slots, first, slab_rows, masks, x, xp, kernels, sums, shift_ops, perm, fine_back, parent_back):
    rows = masks.shape[1]
    width = kernels.shape[1]
    F = perm.shape[0]

    def kernel(
        table, masks, x, xp, kernels, sums, shift, perm, fine_back, parent_back, fine_out, parent_out, acc, rows_out
    ):
        acc[...] = sums[...]
        add_terms(table, slots, first, slab_rows, masks, x, xp, kernels, acc)
        far = [(acc[p, F:, :] * 0.5).astype(jnp.bfloat16) for p in range(8)]
        local = jnp.concatenate(far, axis=0)
        parent_out[...] = moved_rows(parent_back[...], local)
        ordered = moved_rows(perm[...], local)
        near = []
        for p in range(8):
            moved = jnp.dot(ordered, shift[p], preferred_element_type=jnp.float32)
            near.append((acc[p, :F, :] + moved).astype(jnp.bfloat16))
        whole = jnp.dot(fine_back[...], jnp.concatenate(near, axis=1), preferred_element_type=jnp.float32)
        for p in range(8):
            rows_out[:, p, :] = whole[:, p * width : (p + 1) * width]
        fine_out[...] = rows_out[...].reshape(8 * F, width).astype(jnp.bfloat16)

    vmem = pl.BlockSpec(memory_space=pltpu.VMEM)
    return pl.pallas_call(
        kernel,
        out_shape=(
            jax.ShapeDtypeStruct((8 * F, width), jnp.bfloat16),
            jax.ShapeDtypeStruct((8 * (rows - F), width), jnp.bfloat16),
        ),
        in_specs=[pl.BlockSpec(memory_space=pltpu.SMEM)] + [vmem] * 9,
        out_specs=(vmem, vmem),
        scratch_shapes=[pltpu.VMEM((8, rows, width), jnp.float32), pltpu.VMEM((F, 8, width), jnp.float32)],
        compiler_params=pltpu.CompilerParams(vmem_limit_bytes=16 << 20),
        name="last_terms",
    )(table, masks, x, xp, kernels, sums, shift_ops, perm, fine_back, parent_back)


def parent_order(parent_bits):
    count = 2**parent_bits
    held = np.arange(count).reshape(-1, 8)[grid_permutation(parent_bits - 3)].T.reshape(-1)
    place = np.zeros(count, np.int64)
    place[held] = np.arange(count)
    perm = np.zeros((count, count), np.float32)
    perm[np.arange(count), place[grid_permutation(parent_bits)]] = 1
    return perm


def grid_back(total_bits):
    order = np.zeros((2**total_bits, 2**total_bits), np.float32)
    order[grid_permutation(total_bits), np.arange(2**total_bits)] = 1
    return order


def back_order(total_bits):
    count = 2**total_bits
    numbers = np.arange(count).reshape(-1, 8)[grid_permutation(total_bits - 3)].T.reshape(-1)
    order = np.zeros((count, count), np.float32)
    order[numbers, np.arange(count)] = 1
    return order


def on_device(fine_mult, parent_mult, fine_mask, parent_mask, kernels, shift_ops):
    device_bits = lax.axis_size("box").bit_length() - 1
    device_index = lax.axis_index("box")
    fine_bits = fine_mult.shape[0].bit_length() - 1
    parent_bits = parent_mult.shape[0].bit_length() - 1
    width = fine_mult.shape[1]
    words = fine_mask.shape[0]
    fine = octant_grids(fine_mult, fine_bits)
    parent = octant_grids(parent_mult, parent_bits)
    F = fine_mult.shape[0] // 8
    G = parent_mult.shape[0] // 8
    n1, n2, n3 = fine.shape[1:4]
    m1, m2, m3 = parent.shape[1:4]
    is_odd = parity(0, fine_bits, device_index, device_bits)
    lists = shift_lists()
    slots = [126, 72]
    tables = []
    for odd in (False, True):
        near_side, far_side = (0, 2) if odd else (2, 0)
        tables.append(
            (
                work_table([lists[1], lists[near_side]], slots[0], n1 + 2),
                work_table([lists[far_side]], slots[1], n1 + 2),
            )
        )

    def by_parity(make):
        return jnp.where(is_odd, make(tables[1]), make(tables[0]))

    def columns(line):
        def make(pair):
            joined = np.concatenate([pair[0][line], pair[1][line]], axis=1)
            return np.pad(joined, ((0, 0), (0, -joined.shape[1] % 128)))

        return by_parity(make)

    def entries(which):
        def make(pair):
            lengths = (pair[which][1] >= 0).sum(axis=1)
            lead = 0 if lengths[0] > lengths[4] else 4
            assert set(lengths[lead : lead + 4]) == {slots[which]}
            assert set(lengths[4 - lead : 8 - lead]) == {slots[which] - SHORTER}
            return np.concatenate([pair[which][0].reshape(-1), np.array([lead], np.int32)])

        return by_parity(make)

    first_table = entries(0)
    last_table = entries(1)
    fine, parent = exchange(fine, parent, 1, fine_bits, device_index, device_bits)
    fine, parent, fine_mask, parent_mask = lax.optimization_barrier(
        (fine, parent, fine_mask, parent_mask)
    )
    masks = jnp.concatenate(
        [
            octant_grids(fine_mask.T, fine_bits).reshape(8, F, words),
            octant_grids(parent_mask.T, parent_bits).reshape(8, G, words),
        ],
        axis=1,
    )
    packed = jnp.stack([masks & 255, jnp.right_shift(masks, 8)], axis=3).astype(jnp.bfloat16)
    held = unpack_masks(packed.reshape(8, F + G, 2 * words), columns(1), columns(2))
    fine, parent = exchange(fine, parent, 2, fine_bits, device_index, device_bits)
    top = packed_face(fine, parent, 1, True)
    bottom = packed_face(fine, parent, 1, False)
    even_got = lax.ppermute(
        jnp.where(is_odd, bottom, top), "box", pair_route(0, 0, fine_bits, device_bits)
    )
    odd_got = lax.ppermute(
        jnp.where(is_odd, top, bottom), "box", pair_route(0, 1, fine_bits, device_bits)
    )
    split = (n2 + 2) * (n3 + 2)

    def slab(got):
        return got[:, :split].reshape(8, 1, n2 + 2, n3 + 2, width)

    def parent_slab(got):
        return got[:, split:].reshape(8, 1, m2 + 2, m3 + 2, width)

    def across(block, w2, w3):
        return jnp.stack(
            [
                block[:, :, b : b + w2, c : c + w3].reshape(8, -1, width)
                for b in range(3)
                for c in range(3)
            ]
        )

    def moved_parents(got, goes_up):
        slab_got = parent_slab(got)
        up = jnp.concatenate([parent[:, 1:], slab_got], axis=1)
        down = jnp.concatenate([slab_got, parent[:, : m1 - 1]], axis=1)
        return across(jnp.where(goes_up, up, down), m2, m3)

    even = slab(even_got)
    x_even = across(jnp.concatenate([even, fine, even], axis=1), n2, n3)
    xp_even = jnp.concatenate(
        [across(parent, m2, m3), moved_parents(even_got, jnp.logical_not(is_odd))]
    ).reshape(-1, G, width)
    sums = first_terms(first_table, slots[0], n2 * n3, held, x_even.reshape(-1, width), xp_even, kernels)
    sums, odd_got = lax.optimization_barrier((sums, odd_got))
    odd_across = across(slab(odd_got), n2, n3)
    slab_rows = n2 * n3
    x_odd = lax.dynamic_update_slice(x_even, odd_across, (0, 0, 0, 0))
    x_odd = lax.dynamic_update_slice(x_odd, odd_across, (0, 0, (n1 + 1) * slab_rows, 0))
    xp_odd = moved_parents(odd_got, is_odd).reshape(-1, G, width)
    fine_local, parent_local = last_terms(
        last_table,
        slots[1],
        slots[0],
        n2 * n3,
        held,
        x_odd.reshape(-1, width),
        xp_odd,
        kernels,
        sums,
        shift_ops,
        jnp.asarray(parent_order(parent_bits), jnp.bfloat16),
        jnp.asarray(grid_back(parent_bits), jnp.bfloat16),
        jnp.asarray(back_order(parent_bits), jnp.bfloat16),
    )
    return fine_local, parent_local


def solution(mesh):
    return jax.shard_map(
        on_device,
        mesh=mesh,
        in_specs=(P("box", None), P("box", None), P(None, "box"), P(None, "box"), P(), P()),
        out_specs=(P("box", None), P("box", None)),
        check_vma=False,
    )
```
